256 devices in a mesh: row: 8 (over z), col: 32 (over x, y, core).
Axes of the slice: x: 4, y: 4, z: 8, core: 2. Of those that a mesh axis runs over, the one named last changes fastest.
Arguments:
- latitude: bfloat16 [16384, 256], P(('row', 'col')), may hold values from -4 to 4
- longitude: bfloat16 [16384, 512], P(('row', 'col')), may hold values from -4 to 4
- weight: bfloat16 [16384], P(('row', 'col')), may hold values from 0.29882812 to 3
- harmonic_index: int32 [2, 24576], P(None, 'col'), may hold values from 0 to 511, as said below
Outputs:
- coefficients: float32 [512, 24576], P(None, 'col')
- residual: float32 [16384, 24576], P('row', 'col')
The draws below stay inside these ranges and needn't reach their ends.
Inputs may be any that keep to these rules, and one draw needn't show every extreme that they name: The pairs (harmonic_index[0, j], harmonic_index[1, j]) are distinct over all 24576 columns; row 0 is below 256, and harmonic_index[1, j] // 2 never exceeds harmonic_index[0, j].
All inputs are finite; a program needn't handle non-finite values.
Results may differ from the reference program's by a relative error of at most 0.0003.
Values may be sent and summed in bfloat16 or wider, within the bound.
No kernel may reach another device: no remote copies, remote signals or barrier semaphores. Data moves between devices by JAX's collectives and lax.ppermute only.
A program may use at most 128 MiB of HBM per device.

```python
import math
import jax
import jax.numpy as jnp
from jax import lax

COL_DEV = 768
PANEL = 256
NDEG = 256
NORD = 512
EPOCHS = 16384
NCOLS = 24576


def draw_harmonic_index(key, part):
    shuffled = jax.random.permutation(jax.random.fold_in(key, 11), NDEG * NORD).astype(jnp.int32)
    degree_all = shuffled // NORD
    order_all = shuffled % NORD
    invalid = (order_all // 2 > degree_all).astype(jnp.int32)
    ranked = jnp.argsort(invalid, stable=True)
    chosen = shuffled[ranked][:NCOLS]
    return jnp.stack([chosen // NORD, chosen % NORD]).astype(jnp.int32)


def level_of(key, extent, split, least, largest):
    def one(position, shards_of):
        steps = jax.random.uniform(jax.random.fold_in(jax.random.fold_in(key, 6), position), (shards_of,), jnp.float32, least / len(split), largest / len(split))
        return jnp.repeat(jnp.exp(steps), extent[position] // shards_of).reshape((-1,) + (1,) * (len(extent) - position - 1))

    loudness = one(*split[0])
    for cut in split[1:]:
        loudness = loudness * one(*cut)
    return loudness


def noise(key, dims, spread, most, split=(), dtype=jnp.bfloat16):
    entries = jax.random.normal(key, dims, jnp.float32) * spread
    if len(split) > 0:
        entries = level_of(key, dims, split, -0.22, 0.18) * entries
    return jnp.clip(entries, min=-most, max=most).astype(dtype)


def setup_inputs(seed: int = 0) -> dict:
    key_list = jax.random.split(jax.random.key(seed), 5)
    return {
        "latitude": noise(key_list[0], (EPOCHS, NDEG), 1.0, 4.0, ((0, 256),)),
        "longitude": noise(key_list[1], (EPOCHS, NORD), 1.0, 4.0, ((0, 256),)),
        "weight": jnp.clip(jnp.exp(math.log(3.0) - 2.306499 * jax.random.uniform(key_list[2], (EPOCHS,), jnp.float32) ** level_of(key_list[2], (EPOCHS,), ((0, 256),), -0.2, 0.2)), 0.29882812, 3.0).astype(jnp.bfloat16),
        "harmonic_index": draw_harmonic_index(jax.random.fold_in(key_list[4], 71), 0),
    }


def synthesize(latitude, longitude, weight, column_index):
    picked_degree = jnp.take(latitude, column_index[0], axis=1).astype(jnp.float32)
    picked_order = jnp.take(longitude, column_index[1], axis=1).astype(jnp.float32)
    return weight.astype(jnp.float32)[:, None] * picked_degree * picked_order

def reference(latitude, longitude, weight, harmonic_index):
    panel_cols = synthesize(latitude, longitude, weight, harmonic_index[:, :2 * PANEL])
    gram_sum = jnp.dot(panel_cols.T.astype(jnp.float32), panel_cols.astype(jnp.float32), precision=lax.Precision.HIGHEST, preferred_element_type=jnp.float32)
    lower_factor = jnp.linalg.cholesky(gram_sum)
    basis_t = lax.linalg.triangular_solve(lower_factor, panel_cols.T, left_side=True, lower=True)
    blocks = harmonic_index.reshape(2, -1, COL_DEV).transpose(1, 0, 2)

    def per_block(block_index):
        design_block = synthesize(latitude, longitude, weight, block_index)
        top_rows = jnp.dot(basis_t.astype(jnp.float32), design_block.astype(jnp.float32), precision=lax.Precision.HIGHEST, preferred_element_type=jnp.float32)
        rest = design_block - jnp.dot(basis_t.T.astype(jnp.float32), top_rows.astype(jnp.float32), precision=lax.Precision.HIGHEST, preferred_element_type=jnp.float32)
        return (top_rows, rest)
    top_all, rest_all = lax.map(per_block, blocks)
    coefficients = top_all.transpose(1, 0, 2).reshape(2 * PANEL, -1)
    residual = rest_all.transpose(1, 0, 2).reshape(EPOCHS, -1)
    return (coefficients, residual)
```

```python
import functools

import jax
import jax.numpy as jnp
from jax import lax
from jax.experimental import pallas as pl
from jax.experimental.pallas import tpu as pltpu
from jax.sharding import Mesh, PartitionSpec as P

F32 = jnp.float32
BF16 = jnp.bfloat16
NP = 512
NDEG = 256
NORD = 512
TAB = NDEG + NORD
WIDE = TAB + 128
NB = 128
GROUP = 8
HIGHEST = lax.Precision.HIGHEST
VMEM_LIMIT = 28 * 1024 * 1024
SMALL_VMEM = 16 * 1024 * 1024


def dot(a, b, dims=((1,), (0,)), precision=None):
    return lax.dot_general(a, b, (dims, ((), ())), precision=precision, preferred_element_type=F32)


def in_hbm(*arrays):
    return tuple(pltpu.with_memory_space_constraint(x, pltpu.HBM) for x in arrays)


def split(x):
    high = x.astype(BF16)
    return high, (x - high.astype(F32)).astype(BF16)


def pack_kernel(lat_ref, lon_ref, weight_ref, lead_ref, out_ref, flip):
    flip[...] = jnp.zeros_like(flip)
    flip[0:1, 0:64] = weight_ref[...].astype(F32)
    lead = lead_ref[...]
    degree, order = lead[0:1, :], lead[1:2, :]
    half = order >> 1
    for base, row in ((1, degree), (9, half), (17, order - 2 * half)):
        row = row.astype(F32)
        for k in range(NP // 64):
            flip[base + k : base + k + 1, 0:64] = row[:, 64 * k : 64 * (k + 1)]
    tail = flip[...].T[0:64, :].astype(BF16)
    lat, lon = lat_ref[...], lon_ref[...]
    for p in range(out_ref.shape[0]):
        out_ref[p, :, 0:NDEG] = lat
        out_ref[p, :, NDEG:TAB] = lon
        out_ref[p, :, TAB:WIDE] = tail


def pack(latitude, longitude, weight, lead, count):
    epochs = latitude.shape[0]
    return pl.pallas_call(
        pack_kernel,
        out_shape=jax.ShapeDtypeStruct((count, epochs, WIDE), BF16),
        scratch_shapes=[pltpu.VMEM((128, 128), F32)],
        compiler_params=pltpu.CompilerParams(vmem_limit_bytes=SMALL_VMEM),
        name="pack",
    )(*in_hbm(latitude, longitude), weight.reshape(1, -1), lead)


def onehot_kernel(index_ref, deg_ref, order_ref):
    for ref, row in ((deg_ref, 0), (order_ref, 1)):
        wanted = index_ref[row : row + 1, :]
        ref[...] = (lax.broadcasted_iota(jnp.int32, ref.shape, 0) == wanted).astype(BF16)


def onehots(index):
    cols = index.shape[1]
    return pl.pallas_call(
        onehot_kernel,
        out_shape=[jax.ShapeDtypeStruct((NDEG, cols), BF16), jax.ShapeDtypeStruct((NORD, cols), BF16)],
        compiler_params=pltpu.CompilerParams(vmem_limit_bytes=SMALL_VMEM),
        cost_estimate=pl.CostEstimate(flops=TAB * cols, bytes_accessed=2 * TAB * cols, transcendentals=0),
        name="onehots",
    )(index)


def moments_kernel(second, sub, mine_ref, *refs):
    if second:
        table_ref, deg, order, pdeg, pord, cross_in, slice_in = refs[:7]
        cross_ref, slices_ref, design_ref, high_ref, low_ref, total = refs[10:]
    else:
        head_ref, table_ref, deg, order = refs[:4]
        cross_ref, total, design_ref, high_ref, low_ref, pdeg, pord = refs[4:]

    @pl.when(pl.program_id(0) == 0)
    def _():
        if second:
            cross_ref[...] = cross_in[...]
            total[...] = slice_in[...]
            return
        cross_ref[...] = jnp.zeros_like(cross_ref)
        total[...] = jnp.zeros_like(total)
        head = head_ref[0].astype(F32)
        lanes = lax.broadcasted_iota(jnp.int32, (64, NDEG), 1).astype(F32)
        wide = lax.broadcasted_iota(jnp.int32, (64, NORD), 1).astype(F32)
        for k in range(NP // 64):
            d = head[:, 1 + k : 2 + k]
            o = head[:, 9 + k : 10 + k] * 2.0 + head[:, 17 + k : 18 + k]
            pdeg[64 * k : 64 * (k + 1), :] = (d == lanes).astype(BF16)
            pord[64 * k : 64 * (k + 1), :] = (o == wide).astype(BF16)

    part = total.shape[0]
    at = pl.ds(pl.multiple_of(mine_ref[0] * part, part), part)
    last = ((1,), (1,))

    def synthesize(k):
        rows = slice(k * sub, (k + 1) * sub)
        block = slice(k * sub // 64, (k + 1) * sub // 64)

        def columns(lo, hi):
            return table_ref[block, :, lo:hi].reshape(sub, hi - lo)

        lat, lon = columns(0, NDEG), columns(NDEG, TAB)
        weight = columns(TAB, WIDE).astype(F32)[:, 0:1]
        high, low = split(weight * dot(lat, pdeg[...], last) * dot(lon, pord[...], last))
        own = split(weight * dot(lat, pdeg[at, :], last) * dot(lon, pord[at, :], last))
        high_ref[0, rows, :], low_ref[0, rows, :] = high, low
        design = weight * dot(lat, deg[...]) * dot(lon, order[...])
        design_ref[0, rows, :] = design
        return high, low, own, split(design)

    def accumulate(high, low, own, design):
        lhs = jnp.concatenate([high.T, high.T, low.T], axis=1)
        cross_ref[...] += dot(lhs, jnp.concatenate([design[0], design[1], design[0]], axis=0))
        lhs = jnp.concatenate([own[0].T, own[0].T, own[1].T], axis=1)
        total[...] += dot(lhs, jnp.concatenate([high, low, high], axis=0))

    count = high_ref.shape[1] // sub
    ready = synthesize(0)
    for k in range(count):
        following = synthesize(k + 1) if k + 1 < count else None
        accumulate(*ready)
        ready = following
    if second:
        for k in range(slices_ref.shape[0]):
            slices_ref[k] = total[...]


def moments(table, deg, order, mine, part, rows_of, prior=None, rows=512, sub=256):
    epochs, cols = 64 * table.shape[0], deg.shape[1]
    steps = epochs // rows
    second = prior is not None
    half = 1 if second else 0
    whole = lambda i, s: (0, 0)
    along = lambda i, s: (half, i, 0)
    table_spec = pl.BlockSpec((rows // 64, 64, WIDE), lambda i, s: (i, 0, 0))
    fixed = [pl.BlockSpec(x.shape, whole) for x in (deg, order)]
    pdeg_spec, pord_spec = pl.BlockSpec((NP, NDEG), whole), pl.BlockSpec((NP, NORD), whole)
    cross_spec, slice_spec = pl.BlockSpec((NP, cols), whole), pl.BlockSpec((part, NP), whole)
    big_specs = [
        pl.BlockSpec((1, rows, cols), along),
        pl.BlockSpec((1, rows, NP), along),
        pl.BlockSpec((1, rows, NP), along),
    ]
    big_shapes = [
        pltpu.HBM((2, epochs, cols), F32),
        pltpu.HBM((2, epochs, NP), BF16),
        pltpu.HBM((2, epochs, NP), BF16),
    ]
    cross_shape = (pltpu.HBM if second else jax.ShapeDtypeStruct)((NP, cols), F32)
    if second:
        cross, total, design, high, low, pdeg, pord = prior
        args = (table, deg, order, pdeg, pord, cross, total, *in_hbm(design, high, low))
        in_specs = [table_spec, *fixed, pdeg_spec, pord_spec, cross_spec, slice_spec]
        in_specs += [pl.BlockSpec(memory_space=pl.ANY)] * 3
        out_specs = [cross_spec, pl.BlockSpec((rows_of, part, NP), lambda i, s: (0, 0, 0)), *big_specs]
        out_shape = [cross_shape, jax.ShapeDtypeStruct((rows_of, part, NP), F32), *big_shapes]
        scratch = [pltpu.VMEM((part, NP), F32)]
        aliases = {8: 2, 9: 3, 10: 4}
    else:
        args = (table, table, deg, order)
        in_specs = [pl.BlockSpec((1, 64, 128), lambda i, s: (0, 0, TAB // 128)), table_spec, *fixed]
        out_specs = [cross_spec, slice_spec, *big_specs, pdeg_spec, pord_spec]
        out_shape = [
            cross_shape,
            jax.ShapeDtypeStruct((part, NP), F32),
            *big_shapes,
            jax.ShapeDtypeStruct((NP, NDEG), BF16),
            jax.ShapeDtypeStruct((NP, NORD), BF16),
        ]
        scratch, aliases = [], {}
    return pl.pallas_call(
        functools.partial(moments_kernel, second, sub),
        grid_spec=pltpu.PrefetchScalarGridSpec(
            num_scalar_prefetch=1, grid=(steps,), in_specs=in_specs, out_specs=out_specs, scratch_shapes=scratch
        ),
        out_shape=out_shape,
        input_output_aliases=aliases,
        compiler_params=pltpu.CompilerParams(vmem_limit_bytes=VMEM_LIMIT),
        cost_estimate=pl.CostEstimate(
            flops=2 * epochs * (NP + cols) * TAB + 6 * epochs * cols * NP,
            bytes_accessed=epochs * (2 * WIDE + 4 * cols + 4 * NP),
            transcendentals=0,
        ),
        name="moments_second" if second else "moments_first",
    )(mine, *args)


def invert_block(s_ref, t_ref, x_ref):
    full = (GROUP, NB)
    for g in range(NB // GROUP):
        lo = GROUP * g
        rows = [jnp.broadcast_to(s_ref[lo + i : lo + i + 1, :], full) for i in range(GROUP)]
        extra = [jnp.broadcast_to(t_ref[lo + i : lo + i + 1, :], full) for i in range(GROUP)]
        s = [[jnp.broadcast_to(rows[i][:, lo + j : lo + j + 1], full) for j in range(i + 1)] for i in range(GROUP)]
        inv = [None] * GROUP
        mult = [[None] * GROUP for _ in range(GROUP)]
        for p in range(GROUP):
            inv[p] = 1.0 / s[p][p]
            for i in range(p + 1, GROUP):
                mult[i][p] = s[i][p] * inv[p]
            for i in range(p + 1, GROUP):
                for j in range(p + 1, i + 1):
                    s[i][j] = s[i][j] - mult[i][p] * s[j][p]
            for i in range(p + 1, GROUP):
                rows[i] = rows[i] - mult[i][p] * rows[p]
                extra[i] = extra[i] - mult[i][p] * extra[p]
        for i in range(GROUP):
            x_ref[lo + i : lo + i + 1, :] = (lax.rsqrt(s[i][i]) * extra[i])[0:1, :]
        if g == NB // GROUP - 1:
            break
        y = [r * v for r, v in zip(rows, inv)]
        z = [e * v for e, v in zip(extra, inv)]
        for i in range(GROUP - 1, 0, -1):
            for m in range(i):
                y[m] = y[m] - mult[i][m] * y[i]
                z[m] = z[m] - mult[i][m] * z[i]
        for h in range(g + 1, NB // GROUP):
            at = slice(GROUP * h, GROUP * (h + 1))
            tile = s_ref[at, :]
            other = t_ref[at, :]
            for m in range(GROUP):
                col = jnp.broadcast_to(tile[:, lo + m : lo + m + 1], full)
                if m == 0:
                    da, db = col * y[m], col * z[m]
                else:
                    da, db = da + col * y[m], db + col * z[m]
            s_ref[at, :] = tile - da
            t_ref[at, :] = other - db


def factor_kernel(gram_ref, out_ref, a_ref, s_ref, t_ref, x_ref):
    cores, planes, part = gram_ref.shape[:3]
    for p in range(planes):
        for c in range(cores):
            at = part * (cores * p + c)
            a_ref[at : at + part, :] = gram_ref[c, p]
    out_ref[...] = jnp.zeros_like(out_ref)
    unit = (
        lax.broadcasted_iota(jnp.int32, (NB, NB), 0) == lax.broadcasted_iota(jnp.int32, (NB, NB), 1)
    ).astype(F32)
    count = NP // NB

    @pl.loop(0, count)
    def _(k):
        for i in range(count):

            @pl.when(k == i)
            def _():
                at = slice(NB * i, NB * (i + 1))
                s_ref[...] = a_ref[at, at]

        t_ref[...] = unit
        invert_block(s_ref, t_ref, x_ref)
        for i in range(count):

            @pl.when(k == i)
            def _():
                at = slice(NB * i, NB * (i + 1))
                x = x_ref[...]
                out_ref[at, at] = x
                if i > 0:
                    done = slice(0, NB * i)
                    out_ref[at, done] = dot(x, out_ref[at, done], precision=HIGHEST)
                if i < count - 1:
                    rest = slice(NB * (i + 1), NP)
                    upper = dot(x, a_ref[at, rest], precision=HIGHEST)
                    a_ref[rest, rest] -= dot(upper, upper, ((0,), (0,)), HIGHEST)
                    done = slice(0, NB * (i + 1))
                    out_ref[rest, done] -= dot(upper, out_ref[at, done], ((0,), (0,)), HIGHEST)


def inverse_factor(gram):
    return pl.pallas_call(
        factor_kernel,
        out_shape=jax.ShapeDtypeStruct((NP, NP), F32),
        scratch_shapes=[pltpu.VMEM((NP, NP), F32)] + [pltpu.VMEM((NB, NB), F32)] * 3,
        compiler_params=pltpu.CompilerParams(vmem_limit_bytes=SMALL_VMEM),
        cost_estimate=pl.CostEstimate(flops=300_000_000, bytes_accessed=2 * 4 * NP * NP, transcendentals=0),
        name="inverse_factor",
    )(gram)


def basis_kernel(inv_ref, high_ref, low_ref, qhigh_ref, qlow_ref):
    xhigh, xlow = split(inv_ref[...])
    last = ((1,), (1,))
    high = high_ref[0]
    basis = dot(high, xhigh, last) + dot(high, xlow, last) + dot(low_ref[0], xhigh, last)
    qhigh_ref[0], qlow_ref[0] = split(basis)


def basis_of(inv, high, low, rows=512):
    halves, epochs = high.shape[:2]
    spec = pl.BlockSpec((1, rows, NP), lambda h, i: (h, i, 0))
    return pl.pallas_call(
        basis_kernel,
        grid=(halves, epochs // rows),
        in_specs=[pl.BlockSpec((NP, NP), lambda h, i: (0, 0)), spec, spec],
        out_specs=[spec, spec],
        out_shape=[pltpu.HBM(high.shape, BF16)] * 2,
        compiler_params=pltpu.CompilerParams(vmem_limit_bytes=SMALL_VMEM),
        cost_estimate=pl.CostEstimate(
            flops=12 * epochs * NP * NP, bytes_accessed=16 * epochs * NP, transcendentals=0
        ),
        name="basis_of",
    )(inv, *in_hbm(high, low))


def project_kernel(core_ref, inv_ref, cross_ref, high_ref, low_ref, design_ref, coef_ref, rest_ref, chigh, clow):
    @pl.when((pl.program_id(0) == 0) & (pl.program_id(1) == 0))
    def _():
        coef = dot(inv_ref[...], cross_ref[...], precision=HIGHEST)
        coef_ref[...] = coef
        chigh[...], clow[...] = split(coef)

    high = high_ref[0]
    rest = design_ref[0] - (dot(high, chigh[...]) + dot(high, clow[...]) + dot(low_ref[0], chigh[...]))
    rest_ref[...] = rest.reshape(rest_ref.shape)


def project(core, inv, cross, high, low, design, rows=256):
    halves, epochs, cols = design.shape
    whole = lambda h, i, s: (0, 0)
    along = lambda h, i, s: (h, i, 0)
    tall = rows // 64
    return pl.pallas_call(
        project_kernel,
        grid_spec=pltpu.PrefetchScalarGridSpec(
            num_scalar_prefetch=1,
            grid=(halves, epochs // rows),
            in_specs=[
                pl.BlockSpec((NP, NP), whole),
                pl.BlockSpec((NP, cols), whole),
                pl.BlockSpec((1, rows, NP), along),
                pl.BlockSpec((1, rows, NP), along),
                pl.BlockSpec((1, rows, cols), along),
            ],
            out_specs=[
                pl.BlockSpec((NP, cols), whole),
                pl.BlockSpec((tall, 1, 64, cols), lambda h, i, s: (i, (s[0] + h) % 2, 0, 0)),
            ],
            scratch_shapes=[pltpu.VMEM((NP, cols), BF16), pltpu.VMEM((NP, cols), BF16)],
        ),
        out_shape=[
            jax.ShapeDtypeStruct((NP, cols), F32),
            jax.ShapeDtypeStruct((epochs // 64, halves, 64, cols), F32),
        ],
        compiler_params=pltpu.CompilerParams(vmem_limit_bytes=SMALL_VMEM),
        cost_estimate=pl.CostEstimate(
            flops=12 * epochs * cols * NP, bytes_accessed=2 * epochs * (8 * cols + 4 * NP), transcendentals=0
        ),
        name="project",
    )(core, inv, *in_hbm(cross, high, low, design))


def copies(x, count):
    return jnp.broadcast_to(x[None], (count, *x.shape))


def shards(latitude, longitude, weight, harmonic_index):
    plane, cores, nrow = ("x", "y"), lax.axis_size("core"), lax.axis_size("row")
    places = lax.axis_size("x") * lax.axis_size("y")
    core = lax.axis_index("core")
    mine = (lax.axis_index(plane) * cores + core).reshape(1)
    lead = lax.all_gather(harmonic_index[:, :NP], "core")[0]
    packed = pack(latitude, longitude, weight, lead, places)
    deg, order = onehots(harmonic_index)
    own = lax.all_to_all(packed, plane, 0, 0)
    other = lax.ppermute(own, "core", [(k, (k + 1) % cores) for k in range(cores)])
    part = NP // (places * cores)
    first = moments(own, deg, order, mine, part, nrow)
    cross, slices, design, high, low = moments(other, deg, order, mine, part, nrow, first)
    cross = lax.psum(cross, "row")
    summed = lax.all_to_all(slices, "row", 0, 0).sum(0)
    near = lax.all_to_all(copies(summed, places), plane, 0, 0)
    gram = lax.all_to_all(copies(near, cores), "core", 0, 0)
    inv = inverse_factor(gram)
    qhigh, qlow = basis_of(inv, high, low)
    coefficients, rest = project(core.reshape(1), inv, cross, qhigh, qlow, design)
    return coefficients, rest.reshape(-1, rest.shape[-1])


def solution(mesh):
    sizes = dict(mesh.shape)
    side = int(round((sizes["col"] // 2) ** 0.5))
    fine = Mesh(
        mesh.devices.reshape(sizes["row"], side, sizes["col"] // (2 * side), 2), ("row", "x", "y", "core")
    )
    col = ("x", "y", "core")
    every = ("row", *col)
    return jax.shard_map(
        shards,
        mesh=fine,
        in_specs=(P(every, None), P(every, None), P(every), P(None, col)),
        out_specs=(P(None, col), P("row", col)),
        check_vma=False,
    )
```

```python
import functools

import jax
import jax.numpy as jnp
from jax import lax
from jax.experimental import pallas as pl
from jax.experimental.pallas import tpu as pltpu
from jax.sharding import Mesh, PartitionSpec as P

F32 = jnp.float32
BF16 = jnp.bfloat16
NP = 512
NDEG = 256
NORD = 512
TAB = NDEG + NORD
WIDE = TAB + 128
NB = 128
GROUP = 8
HIGHEST = lax.Precision.HIGHEST
VMEM_LIMIT = 28 * 1024 * 1024
SMALL_VMEM = 16 * 1024 * 1024


def dot(a, b, dims=((1,), (0,)), precision=None):
    return lax.dot_general(a, b, (dims, ((), ())), precision=precision, preferred_element_type=F32)


def in_hbm(*arrays):
    return tuple(pltpu.with_memory_space_constraint(x, pltpu.HBM) for x in arrays)


def split(x):
    high = x.astype(BF16)
    return high, (x - high.astype(F32)).astype(BF16)


def pack_kernel(lat_ref, lon_ref, weight_ref, lead_ref, out_ref, flip):
    flip[...] = jnp.zeros_like(flip)
    flip[0:1, 0:64] = weight_ref[...].astype(F32)
    degree, order = lead_ref[0, 0:1, 0:NP], lead_ref[0, 1:2, 0:NP]
    half = order >> 1
    for base, row in ((1, degree), (9, half), (17, order - 2 * half)):
        row = row.astype(F32)
        for k in range(NP // 64):
            flip[base + k : base + k + 1, 0:64] = row[:, 64 * k : 64 * (k + 1)]
    tail = flip[...].T[0:64, :].astype(BF16)
    lat, lon = lat_ref[...], lon_ref[...]
    for p in range(out_ref.shape[0]):
        out_ref[p, :, 0:NDEG] = lat
        out_ref[p, :, NDEG:TAB] = lon
        out_ref[p, :, TAB:WIDE] = tail


def pack(latitude, longitude, weight, lead, count):
    epochs = latitude.shape[0]
    return pl.pallas_call(
        pack_kernel,
        out_shape=jax.ShapeDtypeStruct((count, epochs, WIDE), BF16),
        scratch_shapes=[pltpu.VMEM((128, 128), F32)],
        compiler_params=pltpu.CompilerParams(vmem_limit_bytes=SMALL_VMEM),
        name="pack",
    )(*in_hbm(latitude, longitude, weight.reshape(1, -1)), lead)


def onehot_kernel(index_ref, deg_ref, order_ref):
    for ref, row in ((deg_ref, 0), (order_ref, 1)):
        wanted = index_ref[row : row + 1, :]
        ref[...] = (lax.broadcasted_iota(jnp.int32, ref.shape, 0) == wanted).astype(BF16)


def onehots(index):
    cols = index.shape[1]
    return pl.pallas_call(
        onehot_kernel,
        out_shape=[jax.ShapeDtypeStruct((NDEG, cols), BF16), jax.ShapeDtypeStruct((NORD, cols), BF16)],
        compiler_params=pltpu.CompilerParams(vmem_limit_bytes=SMALL_VMEM),
        cost_estimate=pl.CostEstimate(flops=TAB * cols, bytes_accessed=2 * TAB * cols, transcendentals=0),
        name="onehots",
    )(index)


def moments_kernel(second, sub, *refs):
    if second:
        table_ref, deg, order, pdeg, pord, cross_in = refs[:6]
        cross_ref, design_ref, high_ref, low_ref = refs[9:]
    else:
        head_ref, table_ref, deg, order = refs[:4]
        cross_ref, design_ref, high_ref, low_ref, pdeg, pord = refs[4:]

    @pl.when(pl.program_id(0) == 0)
    def _():
        if second:
            cross_ref[...] = cross_in[...]
            return
        cross_ref[...] = jnp.zeros_like(cross_ref)
        head = head_ref[0].astype(F32)
        lanes = lax.broadcasted_iota(jnp.int32, (64, NDEG), 1).astype(F32)
        wide = lax.broadcasted_iota(jnp.int32, (64, NORD), 1).astype(F32)
        for k in range(NP // 64):
            d = head[:, 1 + k : 2 + k]
            o = head[:, 9 + k : 10 + k] * 2.0 + head[:, 17 + k : 18 + k]
            pdeg[64 * k : 64 * (k + 1), :] = (d == lanes).astype(BF16)
            pord[64 * k : 64 * (k + 1), :] = (o == wide).astype(BF16)

    last = ((1,), (1,))

    def synthesize(k):
        rows = slice(k * sub, (k + 1) * sub)
        block = slice(k * sub // 64, (k + 1) * sub // 64)

        def columns(lo, hi):
            return table_ref[block, :, lo:hi].reshape(sub, hi - lo)

        lat, lon = columns(0, NDEG), columns(NDEG, TAB)
        weight = columns(TAB, WIDE).astype(F32)[:, 0:1]
        high, low = split(weight * dot(lat, pdeg[...], last) * dot(lon, pord[...], last))
        high_ref[0, rows, :], low_ref[0, rows, :] = high, low
        design = weight * dot(lat, deg[...]) * dot(lon, order[...])
        design_ref[0, rows, :] = design
        return high, low, split(design)

    def accumulate(high, low, design):
        lhs = jnp.concatenate([high.T, high.T, low.T], axis=1)
        cross_ref[...] += dot(lhs, jnp.concatenate([design[0], design[1], design[0]], axis=0))

    count = high_ref.shape[1] // sub
    ready = synthesize(0)
    for k in range(count):
        following = synthesize(k + 1) if k + 1 < count else None
        accumulate(*ready)
        ready = following


def moments(table, deg, order, prior=None, rows=512, sub=256):
    epochs, cols = 64 * table.shape[0], deg.shape[1]
    second = prior is not None
    half = 1 if second else 0
    whole = lambda i: (0, 0)
    along = lambda i: (half, i, 0)
    table_spec = pl.BlockSpec((rows // 64, 64, WIDE), lambda i: (i, 0, 0))
    fixed = [pl.BlockSpec(x.shape, whole) for x in (deg, order)]
    panel_specs = [pl.BlockSpec((NP, NDEG), whole), pl.BlockSpec((NP, NORD), whole)]
    cross_spec = pl.BlockSpec((NP, cols), whole)
    big_specs = [pl.BlockSpec((1, rows, width), along) for width in (cols, NP, NP)]
    big_shapes = [
        pltpu.HBM((2, epochs, cols), F32),
        pltpu.HBM((2, epochs, NP), BF16),
        pltpu.HBM((2, epochs, NP), BF16),
    ]
    if second:
        cross, design, high, low, pdeg, pord = prior
        args = (table, deg, order, pdeg, pord, cross, *in_hbm(design, high, low))
        in_specs = [table_spec, *fixed, *panel_specs, cross_spec] + [pl.BlockSpec(memory_space=pl.ANY)] * 3
        out_specs = [cross_spec, *big_specs]
        out_shape = [pltpu.HBM((NP, cols), F32), *big_shapes]
        aliases = {6: 1, 7: 2, 8: 3}
    else:
        args = (table, table, deg, order)
        in_specs = [pl.BlockSpec((1, 64, 128), lambda i: (0, 0, TAB // 128)), table_spec, *fixed]
        out_specs = [cross_spec, *big_specs, *panel_specs]
        out_shape = [
            jax.ShapeDtypeStruct((NP, cols), F32),
            *big_shapes,
            jax.ShapeDtypeStruct((NP, NDEG), BF16),
            jax.ShapeDtypeStruct((NP, NORD), BF16),
        ]
        aliases = {}
    return pl.pallas_call(
        functools.partial(moments_kernel, second, sub),
        grid=(epochs // rows,),
        in_specs=in_specs,
        out_specs=out_specs,
        out_shape=out_shape,
        input_output_aliases=aliases,
        compiler_params=pltpu.CompilerParams(vmem_limit_bytes=VMEM_LIMIT),
        cost_estimate=pl.CostEstimate(
            flops=2 * epochs * (NP + cols) * TAB + 6 * epochs * cols * NP,
            bytes_accessed=epochs * (2 * WIDE + 4 * cols + 4 * NP),
            transcendentals=0,
        ),
        name="moments_second" if second else "moments_first",
    )(*args)


def slices_kernel(mine_ref, high_ref, low_ref, out_ref, total):
    first = (pl.program_id(0) == 0) & (pl.program_id(1) == 0)
    part = total.shape[0]
    row = mine_ref[0] * part + lax.broadcasted_iota(jnp.int32, (NP, part), 1)
    pick = (lax.broadcasted_iota(jnp.int32, (NP, part), 0) == row).astype(BF16)
    high, low = high_ref[0], low_ref[0]
    own_high, own_low = dot(high, pick).astype(BF16), dot(low, pick).astype(BF16)
    lhs = jnp.concatenate([own_high.T, own_high.T, own_low.T], axis=1)
    added = dot(lhs, jnp.concatenate([high, low, high], axis=0))

    @pl.when(first)
    def _():
        total[...] = added

    @pl.when(jnp.logical_not(first))
    def _():
        total[...] += added

    for k in range(out_ref.shape[0]):
        out_ref[k] = total[...]


def gram_slices(mine, high, low, part, count, rows=1024):
    halves, epochs = high.shape[:2]
    spec = pl.BlockSpec((1, rows, NP), lambda h, i, s: (h, i, 0))
    return pl.pallas_call(
        slices_kernel,
        grid_spec=pltpu.PrefetchScalarGridSpec(
            num_scalar_prefetch=1,
            grid=(halves, epochs // rows),
            in_specs=[spec, spec],
            out_specs=pl.BlockSpec((count, part, NP), lambda h, i, s: (0, 0, 0)),
            scratch_shapes=[pltpu.VMEM((part, NP), F32)],
        ),
        out_shape=jax.ShapeDtypeStruct((count, part, NP), F32),
        compiler_params=pltpu.CompilerParams(vmem_limit_bytes=SMALL_VMEM),
        cost_estimate=pl.CostEstimate(
            flops=12 * epochs * part * NP, bytes_accessed=8 * epochs * NP, transcendentals=0
        ),
        name="gram_slices",
    )(mine, *in_hbm(high, low))


def invert_block(s_ref, t_ref, x_ref):
    full = (GROUP, NB)
    for g in range(NB // GROUP):
        lo = GROUP * g
        rows = [jnp.broadcast_to(s_ref[lo + i : lo + i + 1, :], full) for i in range(GROUP)]
        extra = [jnp.broadcast_to(t_ref[lo + i : lo + i + 1, :], full) for i in range(GROUP)]
        s = [[jnp.broadcast_to(rows[i][:, lo + j : lo + j + 1], full) for j in range(i + 1)] for i in range(GROUP)]
        inv = [None] * GROUP
        mult = [[None] * GROUP for _ in range(GROUP)]
        for p in range(GROUP):
            inv[p] = 1.0 / s[p][p]
            for i in range(p + 1, GROUP):
                mult[i][p] = s[i][p] * inv[p]
            for i in range(p + 1, GROUP):
                for j in range(p + 1, i + 1):
                    s[i][j] = s[i][j] - mult[i][p] * s[j][p]
            for i in range(p + 1, GROUP):
                rows[i] = rows[i] - mult[i][p] * rows[p]
                extra[i] = extra[i] - mult[i][p] * extra[p]
        for i in range(GROUP):
            x_ref[lo + i : lo + i + 1, :] = (lax.rsqrt(s[i][i]) * extra[i])[0:1, :]
        if g == NB // GROUP - 1:
            break
        y = [r * v for r, v in zip(rows, inv)]
        z = [e * v for e, v in zip(extra, inv)]
        for i in range(GROUP - 1, 0, -1):
            for m in range(i):
                y[m] = y[m] - mult[i][m] * y[i]
                z[m] = z[m] - mult[i][m] * z[i]
        for h in range(g + 1, NB // GROUP):
            at = slice(GROUP * h, GROUP * (h + 1))
            tile = s_ref[at, :]
            other = t_ref[at, :]
            for m in range(GROUP):
                col = jnp.broadcast_to(tile[:, lo + m : lo + m + 1], full)
                if m == 0:
                    da, db = col * y[m], col * z[m]
                else:
                    da, db = da + col * y[m], db + col * z[m]
            s_ref[at, :] = tile - da
            t_ref[at, :] = other - db


def factor_kernel(gram_ref, out_ref, a_ref, s_ref, t_ref, x_ref):
    cores, planes, part = gram_ref.shape[:3]
    for p in range(planes):
        for c in range(cores):
            at = part * (cores * p + c)
            a_ref[at : at + part, :] = gram_ref[c, p]
    out_ref[...] = jnp.zeros_like(out_ref)
    unit = (
        lax.broadcasted_iota(jnp.int32, (NB, NB), 0) == lax.broadcasted_iota(jnp.int32, (NB, NB), 1)
    ).astype(F32)
    count = NP // NB

    @pl.loop(0, count)
    def _(k):
        for i in range(count):

            @pl.when(k == i)
            def _():
                at = slice(NB * i, NB * (i + 1))
                s_ref[...] = a_ref[at, at]

        t_ref[...] = unit
        invert_block(s_ref, t_ref, x_ref)
        for i in range(count):

            @pl.when(k == i)
            def _():
                at = slice(NB * i, NB * (i + 1))
                x = x_ref[...]
                out_ref[at, at] = x
                if i > 0:
                    done = slice(0, NB * i)
                    out_ref[at, done] = dot(x, out_ref[at, done], precision=HIGHEST)
                if i < count - 1:
                    rest = slice(NB * (i + 1), NP)
                    upper = dot(x, a_ref[at, rest], precision=HIGHEST)
                    a_ref[rest, rest] -= dot(upper, upper, ((0,), (0,)), HIGHEST)
                    done = slice(0, NB * (i + 1))
                    out_ref[rest, done] -= dot(upper, out_ref[at, done], ((0,), (0,)), HIGHEST)


def inverse_factor(gram):
    return pl.pallas_call(
        factor_kernel,
        out_shape=jax.ShapeDtypeStruct((NP, NP), F32),
        scratch_shapes=[pltpu.VMEM((NP, NP), F32)] + [pltpu.VMEM((NB, NB), F32)] * 3,
        compiler_params=pltpu.CompilerParams(vmem_limit_bytes=SMALL_VMEM),
        cost_estimate=pl.CostEstimate(flops=300_000_000, bytes_accessed=2 * 4 * NP * NP, transcendentals=0),
        name="inverse_factor",
    )(gram)


def basis_kernel(inv_ref, high_ref, low_ref, qhigh_ref, qlow_ref, xhigh_ref, xlow_ref):
    @pl.when((pl.program_id(0) == 0) & (pl.program_id(1) == 0))
    def _():
        xhigh_ref[...], xlow_ref[...] = split(inv_ref[...])

    last = ((1,), (1,))
    high, xhigh = high_ref[0], xhigh_ref[...]
    basis = dot(high, xhigh, last) + dot(high, xlow_ref[...], last) + dot(low_ref[0], xhigh, last)
    qhigh_ref[0], qlow_ref[0] = split(basis)


def basis_of(inv, high, low, rows=512):
    halves, epochs = high.shape[:2]
    spec = pl.BlockSpec((1, rows, NP), lambda h, i: (h, i, 0))
    whole = pl.BlockSpec((NP, NP), lambda h, i: (0, 0))
    return pl.pallas_call(
        basis_kernel,
        grid=(halves, epochs // rows),
        in_specs=[whole, spec, spec],
        out_specs=[spec, spec, whole, whole],
        out_shape=[pltpu.VMEM(high.shape, BF16), pltpu.HBM(high.shape, BF16)] + [pltpu.VMEM((NP, NP), BF16)] * 2,
        compiler_params=pltpu.CompilerParams(vmem_limit_bytes=SMALL_VMEM),
        cost_estimate=pl.CostEstimate(
            flops=12 * epochs * NP * NP, bytes_accessed=16 * epochs * NP, transcendentals=0
        ),
        name="basis_of",
    )(inv, *in_hbm(high, low))


def project_kernel(core_ref, xhigh, xlow, qhigh, cross_ref, qlow_ref, design_ref, coef_ref, rest_ref, both):
    h, i = pl.program_id(0), pl.program_id(1)

    @pl.when((h == 0) & (i == 0))
    def _():
        high, low = split(cross_ref[...])
        coef = dot(xhigh[...], high) + dot(xhigh[...], low) + dot(xlow[...], high)
        coef_ref[...] = coef
        both[0:NP, :], both[NP : 2 * NP, :] = split(coef)

    rows = design_ref.shape[1]
    high = qhigh[h, pl.ds(pl.multiple_of(i * rows, rows), rows), :]
    span = dot(jnp.concatenate([high, high], axis=1), both[...]) + dot(qlow_ref[0], both[0:NP, :])
    rest_ref[...] = (design_ref[0] - span).reshape(rest_ref.shape)


def project(core, xhigh, xlow, cross, high, low, design, rows=512):
    halves, epochs, cols = design.shape
    here = pl.BlockSpec(memory_space=pltpu.VMEM)
    whole = pl.BlockSpec((NP, cols), lambda h, i, s: (0, 0))
    along = lambda h, i, s: (h, i, 0)
    return pl.pallas_call(
        project_kernel,
        grid_spec=pltpu.PrefetchScalarGridSpec(
            num_scalar_prefetch=1,
            grid=(halves, epochs // rows),
            in_specs=[
                here,
                here,
                here,
                whole,
                pl.BlockSpec((1, rows, NP), along),
                pl.BlockSpec((1, rows, cols), along),
            ],
            out_specs=[
                whole,
                pl.BlockSpec((rows // 64, 1, 64, cols), lambda h, i, s: (i, (s[0] + h) % 2, 0, 0)),
            ],
            scratch_shapes=[pltpu.VMEM((2 * NP, cols), BF16)],
        ),
        out_shape=[
            jax.ShapeDtypeStruct((NP, cols), F32),
            jax.ShapeDtypeStruct((epochs // 64, halves, 64, cols), F32),
        ],
        compiler_params=pltpu.CompilerParams(vmem_limit_bytes=VMEM_LIMIT),
        cost_estimate=pl.CostEstimate(
            flops=12 * epochs * cols * NP, bytes_accessed=2 * epochs * (8 * cols + 4 * NP), transcendentals=0
        ),
        name="project",
    )(core, xhigh, xlow, high, *in_hbm(cross, low, design))


def copies(x, count):
    return jnp.broadcast_to(x[None], (count, *x.shape))


def shards(latitude, longitude, weight, harmonic_index):
    plane, cores, nrow = ("x", "y"), lax.axis_size("core"), lax.axis_size("row")
    places = lax.axis_size("x") * lax.axis_size("y")
    core = lax.axis_index("core")
    mine = (lax.axis_index(plane) * cores + core).reshape(1)
    lead = lax.all_gather(harmonic_index, "core")
    packed = pack(latitude, longitude, weight, lead, places)
    deg, order = onehots(harmonic_index)
    own = lax.all_to_all(packed, plane, 0, 0)
    other = lax.ppermute(own, "core", [(k, (k + 1) % cores) for k in range(cores)])
    part = NP // (places * cores)
    cross, design, high, low = moments(other, deg, order, moments(own, deg, order))
    cross = lax.psum(cross, "row")
    slices = gram_slices(mine, high, low, part, nrow)
    summed = lax.all_to_all(slices, "row", 0, 0).sum(0)
    near = lax.all_to_all(copies(summed, places), plane, 0, 0)
    gram = lax.all_to_all(copies(near, cores), "core", 0, 0)
    inv = inverse_factor(gram)
    qhigh, qlow, xhigh, xlow = basis_of(inv, high, low)
    coefficients, rest = project(core.reshape(1), xhigh, xlow, cross, qhigh, qlow, design)
    return coefficients, rest.reshape(-1, rest.shape[-1])


def solution(mesh):
    sizes = dict(mesh.shape)
    side = int(round((sizes["col"] // 2) ** 0.5))
    fine = Mesh(
        mesh.devices.reshape(sizes["row"], side, sizes["col"] // (2 * side), 2), ("row", "x", "y", "core")
    )
    col = ("x", "y", "core")
    every = ("row", *col)
    return jax.shard_map(
        shards,
        mesh=fine,
        in_specs=(P(every, None), P(every, None), P(every), P(None, col)),
        out_specs=(P(None, col), P("row", col)),
        check_vma=False,
    )
```

```python
import functools

import jax
import jax.numpy as jnp
from jax import lax
from jax.experimental import pallas as pl
from jax.experimental.pallas import tpu as pltpu
from jax.sharding import Mesh, PartitionSpec as P

F32 = jnp.float32
BF16 = jnp.bfloat16
NP = 512
NDEG = 256
NORD = 512
TAB = NDEG + NORD
WIDE = TAB + 128
NB = 128
GROUP = 8
HIGHEST = lax.Precision.HIGHEST
VMEM_LIMIT = 28 * 1024 * 1024
SMALL_VMEM = 16 * 1024 * 1024


def dot(a, b, dims=((1,), (0,)), precision=None):
    return lax.dot_general(a, b, (dims, ((), ())), precision=precision, preferred_element_type=F32)


def in_hbm(*arrays):
    return tuple(pltpu.with_memory_space_constraint(x, pltpu.HBM) for x in arrays)


def split(x):
    high = x.astype(BF16)
    return high, (x - high.astype(F32)).astype(BF16)


def pack_kernel(lat_ref, lon_ref, weight_ref, lead_ref, out_ref, flip):
    flip[...] = jnp.zeros_like(flip)
    flip[0:1, 0:64] = weight_ref[...].astype(F32)
    degree, order = lead_ref[0, 0:1, 0:NP], lead_ref[0, 1:2, 0:NP]
    half = order >> 1
    for base, row in ((1, degree), (9, half), (17, order - 2 * half)):
        row = row.astype(F32)
        for k in range(NP // 64):
            flip[base + k : base + k + 1, 0:64] = row[:, 64 * k : 64 * (k + 1)]
    tail = flip[...].T[0:64, :].astype(BF16)
    lat, lon = lat_ref[...], lon_ref[...]
    for p in range(out_ref.shape[0]):
        out_ref[p, :, 0:NDEG] = lat
        out_ref[p, :, NDEG:TAB] = lon
        out_ref[p, :, TAB:WIDE] = tail


def pack(latitude, longitude, weight, lead, count):
    epochs = latitude.shape[0]
    return pl.pallas_call(
        pack_kernel,
        out_shape=jax.ShapeDtypeStruct((count, epochs, WIDE), BF16),
        scratch_shapes=[pltpu.VMEM((128, 128), F32)],
        compiler_params=pltpu.CompilerParams(vmem_limit_bytes=SMALL_VMEM),
        name="pack",
    )(*in_hbm(latitude, longitude, weight.reshape(1, -1)), lead)


def onehot_kernel(index_ref, deg_ref, order_ref):
    for ref, row in ((deg_ref, 0), (order_ref, 1)):
        wanted = index_ref[row : row + 1, :]
        ref[...] = (lax.broadcasted_iota(jnp.int32, ref.shape, 0) == wanted).astype(BF16)


def onehots(index):
    cols = index.shape[1]
    return pl.pallas_call(
        onehot_kernel,
        out_shape=[jax.ShapeDtypeStruct((NDEG, cols), BF16), jax.ShapeDtypeStruct((NORD, cols), BF16)],
        compiler_params=pltpu.CompilerParams(vmem_limit_bytes=SMALL_VMEM),
        cost_estimate=pl.CostEstimate(flops=TAB * cols, bytes_accessed=2 * TAB * cols, transcendentals=0),
        name="onehots",
    )(index)


def moments_kernel(second, sub, *refs):
    if second:
        table_ref, deg, order, pdeg, pord, cross_in = refs[:6]
        cross_ref, design_ref, high_ref, low_ref = refs[9:]
    else:
        head_ref, table_ref, deg, order = refs[:4]
        cross_ref, design_ref, high_ref, low_ref, pdeg, pord = refs[4:]

    @pl.when(pl.program_id(0) == 0)
    def _():
        if second:
            cross_ref[...] = cross_in[...]
            return
        cross_ref[...] = jnp.zeros_like(cross_ref)
        head = head_ref[0].astype(F32)
        lanes = lax.broadcasted_iota(jnp.int32, (64, NDEG), 1).astype(F32)
        wide = lax.broadcasted_iota(jnp.int32, (64, NORD), 1).astype(F32)
        for k in range(NP // 64):
            d = head[:, 1 + k : 2 + k]
            o = head[:, 9 + k : 10 + k] * 2.0 + head[:, 17 + k : 18 + k]
            pdeg[64 * k : 64 * (k + 1), :] = (d == lanes).astype(BF16)
            pord[64 * k : 64 * (k + 1), :] = (o == wide).astype(BF16)

    last = ((1,), (1,))

    def synthesize(k):
        rows = slice(k * sub, (k + 1) * sub)
        block = slice(k * sub // 64, (k + 1) * sub // 64)

        def columns(lo, hi):
            return table_ref[block, :, lo:hi].reshape(sub, hi - lo)

        lat, lon = columns(0, NDEG), columns(NDEG, TAB)
        weight = columns(TAB, WIDE).astype(F32)[:, 0:1]
        high, low = split(weight * dot(lat, pdeg[...], last) * dot(lon, pord[...], last))
        high_ref[0, rows, :], low_ref[0, rows, :] = high, low
        design = weight * dot(lat, deg[...]) * dot(lon, order[...])
        design_ref[0, rows, :] = design
        return high, low, split(design)

    def accumulate(high, low, design):
        lhs = jnp.concatenate([high.T, high.T, low.T], axis=1)
        cross_ref[...] += dot(lhs, jnp.concatenate([design[0], design[1], design[0]], axis=0))

    count = high_ref.shape[1] // sub
    ready = synthesize(0)
    for k in range(count):
        following = synthesize(k + 1) if k + 1 < count else None
        accumulate(*ready)
        ready = following


def moments(table, deg, order, prior=None, rows=512, sub=256):
    epochs, cols = 64 * table.shape[0], deg.shape[1]
    second = prior is not None
    half = 1 if second else 0
    whole = lambda i: (0, 0)
    along = lambda i: (half, i, 0)
    table_spec = pl.BlockSpec((rows // 64, 64, WIDE), lambda i: (i, 0, 0))
    fixed = [pl.BlockSpec(x.shape, whole) for x in (deg, order)]
    panel_specs = [pl.BlockSpec((NP, NDEG), whole), pl.BlockSpec((NP, NORD), whole)]
    cross_spec = pl.BlockSpec((NP, cols), whole)
    big_specs = [pl.BlockSpec((1, rows, width), along) for width in (cols, NP, NP)]
    big_shapes = [
        pltpu.HBM((2, epochs, cols), F32),
        pltpu.HBM((2, epochs, NP), BF16),
        pltpu.HBM((2, epochs, NP), BF16),
    ]
    if second:
        cross, design, high, low, pdeg, pord = prior
        args = (table, deg, order, pdeg, pord, cross, *in_hbm(design, high, low))
        in_specs = [table_spec, *fixed, *panel_specs, cross_spec] + [pl.BlockSpec(memory_space=pl.ANY)] * 3
        out_specs = [cross_spec, *big_specs]
        out_shape = [pltpu.HBM((NP, cols), F32), *big_shapes]
        aliases = {6: 1, 7: 2, 8: 3}
    else:
        args = (table, table, deg, order)
        in_specs = [pl.BlockSpec((1, 64, 128), lambda i: (0, 0, TAB // 128)), table_spec, *fixed]
        out_specs = [cross_spec, *big_specs, *panel_specs]
        out_shape = [
            jax.ShapeDtypeStruct((NP, cols), F32),
            *big_shapes,
            jax.ShapeDtypeStruct((NP, NDEG), BF16),
            jax.ShapeDtypeStruct((NP, NORD), BF16),
        ]
        aliases = {}
    return pl.pallas_call(
        functools.partial(moments_kernel, second, sub),
        grid=(epochs // rows,),
        in_specs=in_specs,
        out_specs=out_specs,
        out_shape=out_shape,
        input_output_aliases=aliases,
        compiler_params=pltpu.CompilerParams(vmem_limit_bytes=VMEM_LIMIT),
        cost_estimate=pl.CostEstimate(
            flops=2 * epochs * (NP + cols) * TAB + 6 * epochs * cols * NP,
            bytes_accessed=epochs * (2 * WIDE + 4 * cols + 4 * NP),
            transcendentals=0,
        ),
        name="moments_second" if second else "moments_first",
    )(*args)


def slice_kernel(mine_ref, high_ref, low_ref, out_ref, total):
    first = (pl.program_id(0) == 0) & (pl.program_id(1) == 0)
    part = total.shape[0]
    row = mine_ref[0] * part + lax.broadcasted_iota(jnp.int32, (NP, part), 1)
    pick = (lax.broadcasted_iota(jnp.int32, (NP, part), 0) == row).astype(BF16)
    high, low = high_ref[0], low_ref[0]
    own_high, own_low = dot(high, pick).astype(BF16), dot(low, pick).astype(BF16)
    lhs = jnp.concatenate([own_high.T, own_high.T, own_low.T], axis=1)
    added = dot(lhs, jnp.concatenate([high, low, high], axis=0))

    @pl.when(first)
    def _():
        total[...] = added

    @pl.when(jnp.logical_not(first))
    def _():
        total[...] += added

    out_ref[...] = total[...]


def gram_slice(mine, high, low, part, rows=1024):
    halves, epochs = high.shape[:2]
    spec = pl.BlockSpec((1, rows, NP), lambda h, i, s: (h, i, 0))
    return pl.pallas_call(
        slice_kernel,
        grid_spec=pltpu.PrefetchScalarGridSpec(
            num_scalar_prefetch=1,
            grid=(halves, epochs // rows),
            in_specs=[spec, spec],
            out_specs=pl.BlockSpec((part, NP), lambda h, i, s: (0, 0)),
            scratch_shapes=[pltpu.VMEM((part, NP), F32)],
        ),
        out_shape=jax.ShapeDtypeStruct((part, NP), F32),
        compiler_params=pltpu.CompilerParams(vmem_limit_bytes=SMALL_VMEM),
        cost_estimate=pl.CostEstimate(
            flops=12 * epochs * part * NP, bytes_accessed=8 * epochs * NP, transcendentals=0
        ),
        name="gram_slice",
    )(mine, *in_hbm(high, low))


def invert_block(s_ref, t_ref, x_ref):
    full = (GROUP, NB)
    for g in range(NB // GROUP):
        lo = GROUP * g
        rows = [jnp.broadcast_to(s_ref[lo + i : lo + i + 1, :], full) for i in range(GROUP)]
        extra = [jnp.broadcast_to(t_ref[lo + i : lo + i + 1, :], full) for i in range(GROUP)]
        s = [[jnp.broadcast_to(rows[i][:, lo + j : lo + j + 1], full) for j in range(i + 1)] for i in range(GROUP)]
        inv = [None] * GROUP
        mult = [[None] * GROUP for _ in range(GROUP)]
        for p in range(GROUP):
            inv[p] = 1.0 / s[p][p]
            for i in range(p + 1, GROUP):
                mult[i][p] = s[i][p] * inv[p]
            for i in range(p + 1, GROUP):
                for j in range(p + 1, i + 1):
                    s[i][j] = s[i][j] - mult[i][p] * s[j][p]
            for i in range(p + 1, GROUP):
                rows[i] = rows[i] - mult[i][p] * rows[p]
                extra[i] = extra[i] - mult[i][p] * extra[p]
        for i in range(GROUP):
            x_ref[lo + i : lo + i + 1, :] = (lax.rsqrt(s[i][i]) * extra[i])[0:1, :]
        if g == NB // GROUP - 1:
            break
        y = [r * v for r, v in zip(rows, inv)]
        z = [e * v for e, v in zip(extra, inv)]
        for i in range(GROUP - 1, 0, -1):
            for m in range(i):
                y[m] = y[m] - mult[i][m] * y[i]
                z[m] = z[m] - mult[i][m] * z[i]
        for h in range(g + 1, NB // GROUP):
            at = slice(GROUP * h, GROUP * (h + 1))
            tile = s_ref[at, :]
            other = t_ref[at, :]
            for m in range(GROUP):
                col = jnp.broadcast_to(tile[:, lo + m : lo + m + 1], full)
                if m == 0:
                    da, db = col * y[m], col * z[m]
                else:
                    da, db = da + col * y[m], db + col * z[m]
            s_ref[at, :] = tile - da
            t_ref[at, :] = other - db


def factor_kernel(gram_ref, out_ref, a_ref, s_ref, t_ref, x_ref):
    cores, planes, part = gram_ref.shape[:3]
    for p in range(planes):
        for c in range(cores):
            at = part * (cores * p + c)
            a_ref[at : at + part, :] = gram_ref[c, p]
    out_ref[...] = jnp.zeros_like(out_ref)
    unit = (
        lax.broadcasted_iota(jnp.int32, (NB, NB), 0) == lax.broadcasted_iota(jnp.int32, (NB, NB), 1)
    ).astype(F32)
    count = NP // NB

    @pl.loop(0, count)
    def _(k):
        for i in range(count):

            @pl.when(k == i)
            def _():
                at = slice(NB * i, NB * (i + 1))
                s_ref[...] = a_ref[at, at]

        t_ref[...] = unit
        invert_block(s_ref, t_ref, x_ref)
        for i in range(count):

            @pl.when(k == i)
            def _():
                at = slice(NB * i, NB * (i + 1))
                x = x_ref[...]
                out_ref[at, at] = x
                if i > 0:
                    done = slice(0, NB * i)
                    out_ref[at, done] = dot(x, out_ref[at, done], precision=HIGHEST)
                if i < count - 1:
                    rest = slice(NB * (i + 1), NP)
                    upper = dot(x, a_ref[at, rest], precision=HIGHEST)
                    a_ref[rest, rest] -= dot(upper, upper, ((0,), (0,)), HIGHEST)
                    done = slice(0, NB * (i + 1))
                    out_ref[rest, done] -= dot(upper, out_ref[at, done], ((0,), (0,)), HIGHEST)


def inverse_factor(gram):
    return pl.pallas_call(
        factor_kernel,
        out_shape=jax.ShapeDtypeStruct((NP, NP), F32),
        scratch_shapes=[pltpu.VMEM((NP, NP), F32)] + [pltpu.VMEM((NB, NB), F32)] * 3,
        compiler_params=pltpu.CompilerParams(vmem_limit_bytes=SMALL_VMEM),
        cost_estimate=pl.CostEstimate(flops=300_000_000, bytes_accessed=2 * 4 * NP * NP, transcendentals=0),
        name="inverse_factor",
    )(gram)


def basis_kernel(inv_ref, high_ref, low_ref, qhigh_ref, qlow_ref, xhigh_ref, xlow_ref):
    @pl.when((pl.program_id(0) == 0) & (pl.program_id(1) == 0))
    def _():
        xhigh_ref[...], xlow_ref[...] = split(inv_ref[...])

    last = ((1,), (1,))
    high, xhigh = high_ref[0], xhigh_ref[...]
    basis = dot(high, xhigh, last) + dot(high, xlow_ref[...], last) + dot(low_ref[0], xhigh, last)
    qhigh_ref[0], qlow_ref[0] = split(basis)


def basis_of(inv, high, low, rows=512):
    halves, epochs = high.shape[:2]
    spec = pl.BlockSpec((1, rows, NP), lambda h, i: (h, i, 0))
    whole = pl.BlockSpec((NP, NP), lambda h, i: (0, 0))
    return pl.pallas_call(
        basis_kernel,
        grid=(halves, epochs // rows),
        in_specs=[whole, spec, spec],
        out_specs=[spec, spec, whole, whole],
        out_shape=[pltpu.VMEM(high.shape, BF16), pltpu.HBM(high.shape, BF16)] + [pltpu.VMEM((NP, NP), BF16)] * 2,
        compiler_params=pltpu.CompilerParams(vmem_limit_bytes=SMALL_VMEM),
        cost_estimate=pl.CostEstimate(
            flops=12 * epochs * NP * NP, bytes_accessed=16 * epochs * NP, transcendentals=0
        ),
        name="basis_of",
    )(inv, *in_hbm(high, low))


def project_kernel(core_ref, xhigh, xlow, qhigh, cross_ref, qlow_ref, design_ref, coef_hbm, rest_ref,
                   coef_ref, both, sem):
    h, i = pl.program_id(0), pl.program_id(1)
    put = pltpu.make_async_copy(coef_ref, coef_hbm, sem)

    @pl.when((h == 0) & (i == 0))
    def _():
        high, low = split(cross_ref[...])
        coef = dot(xhigh[...], high) + dot(xhigh[...], low) + dot(xlow[...], high)
        coef_ref[...] = coef
        put.start()
        both[0:NP, :], both[NP : 2 * NP, :] = split(coef)

    rows = design_ref.shape[1]
    high = qhigh[h, pl.ds(pl.multiple_of(i * rows, rows), rows), :]
    span = dot(jnp.concatenate([high, high], axis=1), both[...]) + dot(qlow_ref[0], both[0:NP, :])
    rest_ref[...] = (design_ref[0] - span).reshape(rest_ref.shape)

    @pl.when((h == pl.num_programs(0) - 1) & (i == pl.num_programs(1) - 1))
    def _():
        put.wait()


def project(core, xhigh, xlow, cross, high, low, design, rows=512):
    halves, epochs, cols = design.shape
    here = pl.BlockSpec(memory_space=pltpu.VMEM)
    whole = pl.BlockSpec((NP, cols), lambda h, i, s: (0, 0))
    along = lambda h, i, s: (h, i, 0)
    return pl.pallas_call(
        project_kernel,
        grid_spec=pltpu.PrefetchScalarGridSpec(
            num_scalar_prefetch=1,
            grid=(halves, epochs // rows),
            in_specs=[
                here,
                here,
                here,
                whole,
                pl.BlockSpec((1, rows, NP), along),
                pl.BlockSpec((1, rows, cols), along),
            ],
            out_specs=[
                pl.BlockSpec(memory_space=pl.ANY),
                pl.BlockSpec((rows // 64, 1, 64, cols), lambda h, i, s: (i, (s[0] + h) % 2, 0, 0)),
            ],
            scratch_shapes=[
                pltpu.VMEM((NP, cols), F32),
                pltpu.VMEM((2 * NP, cols), BF16),
                pltpu.SemaphoreType.DMA,
            ],
        ),
        out_shape=[
            pltpu.HBM((NP, cols), F32),
            jax.ShapeDtypeStruct((epochs // 64, halves, 64, cols), F32),
        ],
        compiler_params=pltpu.CompilerParams(vmem_limit_bytes=VMEM_LIMIT),
        cost_estimate=pl.CostEstimate(
            flops=12 * epochs * cols * NP, bytes_accessed=2 * epochs * (8 * cols + 4 * NP), transcendentals=0
        ),
        name="project",
    )(core, xhigh, xlow, high, *in_hbm(cross, low, design))


def copies(x, count):
    return jnp.broadcast_to(x[None], (count, *x.shape))


def shards(latitude, longitude, weight, harmonic_index):
    plane, cores, nrow = ("x", "y"), lax.axis_size("core"), lax.axis_size("row")
    places = lax.axis_size("x") * lax.axis_size("y")
    core = lax.axis_index("core")
    mine = (lax.axis_index(plane) * cores + core).reshape(1)
    lead = lax.all_gather(harmonic_index, "core")
    packed = pack(latitude, longitude, weight, lead, places)
    deg, order = onehots(harmonic_index)
    own = lax.all_to_all(packed, plane, 0, 0)
    other = lax.ppermute(own, "core", [(k, (k + 1) % cores) for k in range(cores)])
    part = NP // (places * cores)
    cross, design, high, low = moments(other, deg, order, moments(own, deg, order))
    cross = lax.psum(cross, "row")
    summed = gram_slice(mine, high, low, part)
    hop = 1
    while hop < nrow:
        summed = summed + lax.ppermute(summed, "row", [(k, k ^ hop) for k in range(nrow)])
        hop *= 2
    near = lax.all_to_all(copies(summed, places), plane, 0, 0)
    gram = lax.all_to_all(copies(near, cores), "core", 0, 0)
    inv = inverse_factor(gram)
    qhigh, qlow, xhigh, xlow = basis_of(inv, high, low)
    coefficients, rest = project(core.reshape(1), xhigh, xlow, cross, qhigh, qlow, design)
    return coefficients, rest.reshape(-1, rest.shape[-1])


def solution(mesh):
    sizes = dict(mesh.shape)
    side = int(round((sizes["col"] // 2) ** 0.5))
    fine = Mesh(
        mesh.devices.reshape(sizes["row"], side, sizes["col"] // (2 * side), 2), ("row", "x", "y", "core")
    )
    col = ("x", "y", "core")
    every = ("row", *col)
    return jax.shard_map(
        shards,
        mesh=fine,
        in_specs=(P(every, None), P(every, None), P(every), P(None, col)),
        out_specs=(P(None, col), P("row", col)),
        check_vma=False,
    )
```

```python
import functools

import jax
import jax.numpy as jnp
from jax import lax
from jax.experimental import pallas as pl
from jax.experimental.pallas import tpu as pltpu
from jax.sharding import Mesh, PartitionSpec as P

F32 = jnp.float32
BF16 = jnp.bfloat16
NP = 512
NDEG = 256
NORD = 512
TAB = NDEG + NORD
WIDE = TAB + 128
NB = 128
GROUP = 8
HIGHEST = lax.Precision.HIGHEST
VMEM_LIMIT = 28 * 1024 * 1024
SMALL_VMEM = 16 * 1024 * 1024


def dot(a, b, dims=((1,), (0,)), precision=None):
    return lax.dot_general(a, b, (dims, ((), ())), precision=precision, preferred_element_type=F32)


def in_hbm(*arrays):
    return tuple(pltpu.with_memory_space_constraint(x, pltpu.HBM) for x in arrays)


def split(x):
    high = x.astype(BF16)
    return high, (x - high.astype(F32)).astype(BF16)


def pack_kernel(lat_ref, lon_ref, weight_ref, lead_ref, out_ref, flip):
    flip[...] = jnp.zeros_like(flip)
    flip[0:1, 0:64] = weight_ref[...].astype(F32)
    degree, order = lead_ref[0, 0:1, 0:NP], lead_ref[0, 1:2, 0:NP]
    half = order >> 1
    for base, row in ((1, degree), (9, half), (17, order - 2 * half)):
        row = row.astype(F32)
        for k in range(NP // 64):
            flip[base + k : base + k + 1, 0:64] = row[:, 64 * k : 64 * (k + 1)]
    tail = flip[...].T[0:64, :].astype(BF16)
    lat, lon = lat_ref[...], lon_ref[...]
    for p in range(out_ref.shape[0]):
        out_ref[p, :, 0:NDEG] = lat
        out_ref[p, :, NDEG:TAB] = lon
        out_ref[p, :, TAB:WIDE] = tail


def pack(latitude, longitude, weight, lead, count):
    epochs = latitude.shape[0]
    return pl.pallas_call(
        pack_kernel,
        out_specs=pl.BlockSpec(memory_space=pltpu.VMEM),
        out_shape=pltpu.VMEM((count, epochs, WIDE), BF16),
        scratch_shapes=[pltpu.VMEM((128, 128), F32)],
        compiler_params=pltpu.CompilerParams(vmem_limit_bytes=SMALL_VMEM),
        name="pack",
    )(*in_hbm(latitude, longitude, weight.reshape(1, -1)), lead)


def onehot_kernel(index_ref, deg_ref, order_ref):
    for ref, row in ((deg_ref, 0), (order_ref, 1)):
        wanted = index_ref[row : row + 1, :]
        ref[...] = (lax.broadcasted_iota(jnp.int32, ref.shape, 0) == wanted).astype(BF16)


def onehots(index):
    cols = index.shape[1]
    return pl.pallas_call(
        onehot_kernel,
        out_shape=[jax.ShapeDtypeStruct((NDEG, cols), BF16), jax.ShapeDtypeStruct((NORD, cols), BF16)],
        compiler_params=pltpu.CompilerParams(vmem_limit_bytes=SMALL_VMEM),
        cost_estimate=pl.CostEstimate(flops=TAB * cols, bytes_accessed=2 * TAB * cols, transcendentals=0),
        name="onehots",
    )(index)


def moments_kernel(second, sub, *refs):
    if second:
        table_ref, deg, order, pdeg, pord, cross_in = refs[:6]
        cross_ref, design_ref, high_ref, low_ref = refs[9:]
    else:
        table_ref, deg, order = refs[:3]
        cross_ref, design_ref, high_ref, low_ref, pdeg, pord = refs[3:]

    @pl.when(pl.program_id(0) == 0)
    def _():
        if second:
            cross_ref[...] = cross_in[...]
            return
        cross_ref[...] = jnp.zeros_like(cross_ref)
        head = table_ref[0, :, TAB:WIDE].astype(F32)
        lanes = lax.broadcasted_iota(jnp.int32, (64, NDEG), 1).astype(F32)
        wide = lax.broadcasted_iota(jnp.int32, (64, NORD), 1).astype(F32)
        for k in range(NP // 64):
            d = head[:, 1 + k : 2 + k]
            o = head[:, 9 + k : 10 + k] * 2.0 + head[:, 17 + k : 18 + k]
            pdeg[64 * k : 64 * (k + 1), :] = (d == lanes).astype(BF16)
            pord[64 * k : 64 * (k + 1), :] = (o == wide).astype(BF16)

    last = ((1,), (1,))
    count = high_ref.shape[1] // sub

    def synthesize(k):
        rows = slice(k * sub, (k + 1) * sub)
        block = pl.ds((pl.program_id(0) * count + k) * (sub // 64), sub // 64)

        def columns(lo, hi):
            return table_ref[block, :, lo:hi].reshape(sub, hi - lo)

        lat, lon = columns(0, NDEG), columns(NDEG, TAB)
        weight = columns(TAB, WIDE).astype(F32)[:, 0:1]
        high, low = split(weight * dot(lat, pdeg[...], last) * dot(lon, pord[...], last))
        high_ref[0, rows, :], low_ref[0, rows, :] = high, low
        design = weight * dot(lat, deg[...]) * dot(lon, order[...])
        design_ref[0, rows, :] = design
        return high, low, split(design)

    def accumulate(high, low, design):
        lhs = jnp.concatenate([high.T, high.T, low.T], axis=1)
        cross_ref[...] += dot(lhs, jnp.concatenate([design[0], design[1], design[0]], axis=0))

    ready = synthesize(0)
    for k in range(count):
        following = synthesize(k + 1) if k + 1 < count else None
        accumulate(*ready)
        ready = following


def moments(table, deg, order, prior=None, rows=512, sub=256):
    epochs, cols = 64 * table.shape[0], deg.shape[1]
    second = prior is not None
    half = 1 if second else 0
    whole = lambda i: (0, 0)
    along = lambda i: (half, i, 0)
    here = pl.BlockSpec(memory_space=pltpu.VMEM)
    big_specs = [pl.BlockSpec((1, rows, width), along) for width in (cols, NP, NP)]
    big_shapes = [
        pltpu.HBM((2, epochs, cols), F32),
        pltpu.HBM((2, epochs, NP), BF16),
        pltpu.HBM((2, epochs, NP), BF16),
    ]
    if second:
        cross, design, high, low, pdeg, pord = prior
        args = (table, deg, order, pdeg, pord, cross, *in_hbm(design, high, low))
        in_specs = [here] * 6 + [pl.BlockSpec(memory_space=pl.ANY)] * 3
        out_specs = [pl.BlockSpec((NP, cols), whole), *big_specs]
        out_shape = [pltpu.HBM((NP, cols), F32), *big_shapes]
        aliases = {6: 1, 7: 2, 8: 3}
    else:
        args = (table, deg, order)
        in_specs = [here] * 3
        out_specs = [here, *big_specs, here, here]
        out_shape = [
            pltpu.VMEM((NP, cols), F32),
            *big_shapes,
            pltpu.VMEM((NP, NDEG), BF16),
            pltpu.VMEM((NP, NORD), BF16),
        ]
        aliases = {}
    return pl.pallas_call(
        functools.partial(moments_kernel, second, sub),
        grid=(epochs // rows,),
        in_specs=in_specs,
        out_specs=out_specs,
        out_shape=out_shape,
        input_output_aliases=aliases,
        compiler_params=pltpu.CompilerParams(vmem_limit_bytes=VMEM_LIMIT),
        cost_estimate=pl.CostEstimate(
            flops=2 * epochs * (NP + cols) * TAB + 6 * epochs * cols * NP,
            bytes_accessed=epochs * (2 * WIDE + 4 * cols + 4 * NP),
            transcendentals=0,
        ),
        name="moments_second" if second else "moments_first",
    )(*args)


def slice_kernel(mine_ref, high_ref, low_ref, out_ref, total):
    first = (pl.program_id(0) == 0) & (pl.program_id(1) == 0)
    part = total.shape[0]
    row = mine_ref[0] * part + lax.broadcasted_iota(jnp.int32, (NP, part), 1)
    pick = (lax.broadcasted_iota(jnp.int32, (NP, part), 0) == row).astype(BF16)
    high, low = high_ref[0], low_ref[0]
    own_high, own_low = dot(high, pick).astype(BF16), dot(low, pick).astype(BF16)
    lhs = jnp.concatenate([own_high.T, own_high.T, own_low.T], axis=1)
    added = dot(lhs, jnp.concatenate([high, low, high], axis=0))

    @pl.when(first)
    def _():
        total[...] = added

    @pl.when(jnp.logical_not(first))
    def _():
        total[...] += added

    out_ref[...] = total[...]


def gram_slice(mine, high, low, part, rows=1024):
    halves, epochs = high.shape[:2]
    spec = pl.BlockSpec((1, rows, NP), lambda h, i, s: (h, i, 0))
    return pl.pallas_call(
        slice_kernel,
        grid_spec=pltpu.PrefetchScalarGridSpec(
            num_scalar_prefetch=1,
            grid=(halves, epochs // rows),
            in_specs=[spec, spec],
            out_specs=pl.BlockSpec((part, NP), lambda h, i, s: (0, 0)),
            scratch_shapes=[pltpu.VMEM((part, NP), F32)],
        ),
        out_shape=jax.ShapeDtypeStruct((part, NP), F32),
        compiler_params=pltpu.CompilerParams(vmem_limit_bytes=SMALL_VMEM),
        cost_estimate=pl.CostEstimate(
            flops=12 * epochs * part * NP, bytes_accessed=8 * epochs * NP, transcendentals=0
        ),
        name="gram_slice",
    )(mine, *in_hbm(high, low))


def invert_block(s_ref, t_ref, x_ref):
    full = (GROUP, NB)
    for g in range(NB // GROUP):
        lo = GROUP * g
        rows = [jnp.broadcast_to(s_ref[lo + i : lo + i + 1, :], full) for i in range(GROUP)]
        extra = [jnp.broadcast_to(t_ref[lo + i : lo + i + 1, :], full) for i in range(GROUP)]
        s = [[jnp.broadcast_to(rows[i][:, lo + j : lo + j + 1], full) for j in range(i + 1)] for i in range(GROUP)]
        inv = [None] * GROUP
        mult = [[None] * GROUP for _ in range(GROUP)]
        for p in range(GROUP):
            inv[p] = 1.0 / s[p][p]
            for i in range(p + 1, GROUP):
                mult[i][p] = s[i][p] * inv[p]
            for i in range(p + 1, GROUP):
                for j in range(p + 1, i + 1):
                    s[i][j] = s[i][j] - mult[i][p] * s[j][p]
            for i in range(p + 1, GROUP):
                rows[i] = rows[i] - mult[i][p] * rows[p]
                extra[i] = extra[i] - mult[i][p] * extra[p]
        for i in range(GROUP):
            x_ref[lo + i : lo + i + 1, :] = (lax.rsqrt(s[i][i]) * extra[i])[0:1, :]
        if g == NB // GROUP - 1:
            break
        y = [r * v for r, v in zip(rows, inv)]
        z = [e * v for e, v in zip(extra, inv)]
        for i in range(GROUP - 1, 0, -1):
            for m in range(i):
                y[m] = y[m] - mult[i][m] * y[i]
                z[m] = z[m] - mult[i][m] * z[i]
        for h in range(g + 1, NB // GROUP):
            at = slice(GROUP * h, GROUP * (h + 1))
            tile = s_ref[at, :]
            other = t_ref[at, :]
            for m in range(GROUP):
                col = jnp.broadcast_to(tile[:, lo + m : lo + m + 1], full)
                if m == 0:
                    da, db = col * y[m], col * z[m]
                else:
                    da, db = da + col * y[m], db + col * z[m]
            s_ref[at, :] = tile - da
            t_ref[at, :] = other - db


def factor_kernel(gram_ref, out_ref, a_ref, s_ref, t_ref, x_ref):
    cores, planes, part = gram_ref.shape[:3]
    for p in range(planes):
        for c in range(cores):
            at = part * (cores * p + c)
            a_ref[at : at + part, :] = gram_ref[c, p]
    out_ref[...] = jnp.zeros_like(out_ref)
    unit = (
        lax.broadcasted_iota(jnp.int32, (NB, NB), 0) == lax.broadcasted_iota(jnp.int32, (NB, NB), 1)
    ).astype(F32)
    count = NP // NB

    @pl.loop(0, count)
    def _(k):
        for i in range(count):

            @pl.when(k == i)
            def _():
                at = slice(NB * i, NB * (i + 1))
                s_ref[...] = a_ref[at, at]

        t_ref[...] = unit
        invert_block(s_ref, t_ref, x_ref)
        for i in range(count):

            @pl.when(k == i)
            def _():
                at = slice(NB * i, NB * (i + 1))
                x = x_ref[...]
                out_ref[at, at] = x
                if i > 0:
                    done = slice(0, NB * i)
                    out_ref[at, done] = dot(x, out_ref[at, done], precision=HIGHEST)
                if i < count - 1:
                    rest = slice(NB * (i + 1), NP)
                    upper = dot(x, a_ref[at, rest], precision=HIGHEST)
                    a_ref[rest, rest] -= dot(upper, upper, ((0,), (0,)), HIGHEST)
                    done = slice(0, NB * (i + 1))
                    out_ref[rest, done] -= dot(upper, out_ref[at, done], ((0,), (0,)), HIGHEST)


def inverse_factor(gram):
    return pl.pallas_call(
        factor_kernel,
        out_shape=jax.ShapeDtypeStruct((NP, NP), F32),
        scratch_shapes=[pltpu.VMEM((NP, NP), F32)] + [pltpu.VMEM((NB, NB), F32)] * 3,
        compiler_params=pltpu.CompilerParams(vmem_limit_bytes=SMALL_VMEM),
        cost_estimate=pl.CostEstimate(flops=300_000_000, bytes_accessed=2 * 4 * NP * NP, transcendentals=0),
        name="inverse_factor",
    )(gram)


def basis_kernel(inv_ref, high_ref, low_ref, qhigh_ref, qlow_ref, xhigh_ref, xlow_ref):
    @pl.when((pl.program_id(0) == 0) & (pl.program_id(1) == 0))
    def _():
        xhigh_ref[...], xlow_ref[...] = split(inv_ref[...])

    last = ((1,), (1,))
    high, xhigh = high_ref[0], xhigh_ref[...]
    basis = dot(high, xhigh, last) + dot(high, xlow_ref[...], last) + dot(low_ref[0], xhigh, last)
    qhigh_ref[0], qlow_ref[0] = split(basis)


def basis_of(inv, high, low, rows=512):
    halves, epochs = high.shape[:2]
    spec = pl.BlockSpec((1, rows, NP), lambda h, i: (h, i, 0))
    whole = pl.BlockSpec((NP, NP), lambda h, i: (0, 0))
    return pl.pallas_call(
        basis_kernel,
        grid=(halves, epochs // rows),
        in_specs=[whole, spec, spec],
        out_specs=[spec, spec, whole, whole],
        out_shape=[pltpu.VMEM(high.shape, BF16), pltpu.HBM(high.shape, BF16)] + [pltpu.VMEM((NP, NP), BF16)] * 2,
        compiler_params=pltpu.CompilerParams(vmem_limit_bytes=SMALL_VMEM),
        cost_estimate=pl.CostEstimate(
            flops=12 * epochs * NP * NP, bytes_accessed=16 * epochs * NP, transcendentals=0
        ),
        name="basis_of",
    )(inv, *in_hbm(high, low))


def project_kernel(core_ref, xhigh, xlow, qhigh, cross_ref, qlow_ref, design_ref, coef_hbm, rest_ref,
                   coef_ref, both, sem):
    h, i = pl.program_id(0), pl.program_id(1)
    put = pltpu.make_async_copy(coef_ref, coef_hbm, sem)

    @pl.when((h == 0) & (i == 0))
    def _():
        high, low = split(cross_ref[...])
        half = NP // 2
        for rows, depth in ((slice(0, half), half), (slice(half, NP), NP)):
            left = [x[rows, 0:depth] for x in (xhigh, xhigh, xlow)]
            right = [x[0:depth] for x in (high, low, high)]
            coef_ref[rows, :] = dot(jnp.concatenate(left, axis=1), jnp.concatenate(right, axis=0))
        put.start()
        both[0:NP, :], both[NP : 2 * NP, :] = split(coef_ref[...])

    rows = design_ref.shape[1]
    high = qhigh[h, pl.ds(pl.multiple_of(i * rows, rows), rows), :]
    span = dot(jnp.concatenate([high, high], axis=1), both[...]) + dot(qlow_ref[0], both[0:NP, :])
    rest_ref[...] = (design_ref[0] - span).reshape(rest_ref.shape)

    @pl.when((h == pl.num_programs(0) - 1) & (i == pl.num_programs(1) - 1))
    def _():
        put.wait()


def project(core, xhigh, xlow, cross, high, low, design, rows=512):
    halves, epochs, cols = design.shape
    here = pl.BlockSpec(memory_space=pltpu.VMEM)
    whole = pl.BlockSpec((NP, cols), lambda h, i, s: (0, 0))
    along = lambda h, i, s: (h, i, 0)
    return pl.pallas_call(
        project_kernel,
        grid_spec=pltpu.PrefetchScalarGridSpec(
            num_scalar_prefetch=1,
            grid=(halves, epochs // rows),
            in_specs=[
                here,
                here,
                here,
                whole,
                pl.BlockSpec((1, rows, NP), along),
                pl.BlockSpec((1, rows, cols), along),
            ],
            out_specs=[
                pl.BlockSpec(memory_space=pl.ANY),
                pl.BlockSpec((rows // 64, 1, 64, cols), lambda h, i, s: (i, (s[0] + h) % 2, 0, 0)),
            ],
            scratch_shapes=[
                pltpu.VMEM((NP, cols), F32),
                pltpu.VMEM((2 * NP, cols), BF16),
                pltpu.SemaphoreType.DMA,
            ],
        ),
        out_shape=[
            pltpu.HBM((NP, cols), F32),
            jax.ShapeDtypeStruct((epochs // 64, halves, 64, cols), F32),
        ],
        compiler_params=pltpu.CompilerParams(vmem_limit_bytes=VMEM_LIMIT),
        cost_estimate=pl.CostEstimate(
            flops=12 * epochs * cols * NP, bytes_accessed=2 * epochs * (8 * cols + 4 * NP), transcendentals=0
        ),
        name="project",
    )(core, xhigh, xlow, high, *in_hbm(cross, low, design))


def copies(x, count):
    return jnp.broadcast_to(x[None], (count, *x.shape))


def shards(latitude, longitude, weight, harmonic_index):
    plane, cores, nrow = ("x", "y"), lax.axis_size("core"), lax.axis_size("row")
    places = lax.axis_size("x") * lax.axis_size("y")
    core = lax.axis_index("core")
    mine = (lax.axis_index(plane) * cores + core).reshape(1)
    lead = lax.all_gather(harmonic_index, "core")
    packed = pack(latitude, longitude, weight, lead, places)
    deg, order = onehots(harmonic_index)
    own = lax.all_to_all(packed, plane, 0, 0)
    other = lax.ppermute(own, "core", [(k, (k + 1) % cores) for k in range(cores)])
    part = NP // (places * cores)
    cross, design, high, low = moments(other, deg, order, moments(own, deg, order))
    cross = lax.psum(cross, "row")
    summed = gram_slice(mine, high, low, part)
    hop = 1
    while hop < nrow:
        summed = summed + lax.ppermute(summed, "row", [(k, k ^ hop) for k in range(nrow)])
        hop *= 2
    near = lax.all_to_all(copies(summed, places), plane, 0, 0)
    gram = lax.all_to_all(copies(near, cores), "core", 0, 0)
    inv = inverse_factor(gram)
    qhigh, qlow, xhigh, xlow = basis_of(inv, high, low)
    coefficients, rest = project(core.reshape(1), xhigh, xlow, cross, qhigh, qlow, design)
    return coefficients, rest.reshape(-1, rest.shape[-1])


def solution(mesh):
    sizes = dict(mesh.shape)
    side = int(round((sizes["col"] // 2) ** 0.5))
    fine = Mesh(
        mesh.devices.reshape(sizes["row"], side, sizes["col"] // (2 * side), 2), ("row", "x", "y", "core")
    )
    col = ("x", "y", "core")
    every = ("row", *col)
    return jax.shard_map(
        shards,
        mesh=fine,
        in_specs=(P(every, None), P(every, None), P(every), P(None, col)),
        out_specs=(P(None, col), P("row", col)),
        check_vma=False,
    )
```

```python
import functools

import jax
import jax.numpy as jnp
from jax import lax
from jax.experimental import pallas as pl
from jax.experimental.pallas import tpu as pltpu
from jax.sharding import Mesh, PartitionSpec as P

F32 = jnp.float32
BF16 = jnp.bfloat16
NP = 512
NDEG = 256
NORD = 512
TAB = NDEG + NORD
WIDE = TAB + 128
NB = 128
GROUP = 8
HIGHEST = lax.Precision.HIGHEST
VMEM_LIMIT = 28 * 1024 * 1024
SMALL_VMEM = 16 * 1024 * 1024


def dot(a, b, dims=((1,), (0,)), precision=None):
    return lax.dot_general(a, b, (dims, ((), ())), precision=precision, preferred_element_type=F32)


def in_hbm(*arrays):
    return tuple(pltpu.with_memory_space_constraint(x, pltpu.HBM) for x in arrays)


def split(x):
    high = x.astype(BF16)
    return high, (x - high.astype(F32)).astype(BF16)


def pack_kernel(lat_ref, lon_ref, weight_ref, lead_ref, out_ref, flip):
    flip[...] = jnp.zeros_like(flip)
    flip[0:1, 0:64] = weight_ref[...].astype(F32)
    degree, order = lead_ref[0, 0:1, 0:NP], lead_ref[0, 1:2, 0:NP]
    half = order >> 1
    for base, row in ((1, degree), (9, half), (17, order - 2 * half)):
        row = row.astype(F32)
        for k in range(NP // 64):
            flip[base + k : base + k + 1, 0:64] = row[:, 64 * k : 64 * (k + 1)]
    tail = flip[...].T[0:64, :].astype(BF16)
    lat, lon = lat_ref[...], lon_ref[...]
    for p in range(out_ref.shape[0]):
        out_ref[p, :, 0:NDEG] = lat
        out_ref[p, :, NDEG:TAB] = lon
        out_ref[p, :, TAB:WIDE] = tail


def pack(latitude, longitude, weight, lead, count):
    epochs = latitude.shape[0]
    return pl.pallas_call(
        pack_kernel,
        out_specs=pl.BlockSpec(memory_space=pltpu.VMEM),
        out_shape=pltpu.VMEM((count, epochs, WIDE), BF16),
        scratch_shapes=[pltpu.VMEM((128, 128), F32)],
        compiler_params=pltpu.CompilerParams(vmem_limit_bytes=SMALL_VMEM),
        name="pack",
    )(*in_hbm(latitude, longitude, weight.reshape(1, -1)), lead)


def onehot_kernel(index_ref, deg_ref, order_ref):
    for ref, row in ((deg_ref, 0), (order_ref, 1)):
        wanted = index_ref[row : row + 1, :]
        ref[...] = (lax.broadcasted_iota(jnp.int32, ref.shape, 0) == wanted).astype(BF16)


def onehots(index):
    cols = index.shape[1]
    return pl.pallas_call(
        onehot_kernel,
        out_shape=[jax.ShapeDtypeStruct((NDEG, cols), BF16), jax.ShapeDtypeStruct((NORD, cols), BF16)],
        compiler_params=pltpu.CompilerParams(vmem_limit_bytes=SMALL_VMEM),
        cost_estimate=pl.CostEstimate(flops=TAB * cols, bytes_accessed=2 * TAB * cols, transcendentals=0),
        name="onehots",
    )(index)


def moments_kernel(second, sub, *refs):
    if second:
        table_ref, deg, order, pdeg, pord, cross_in = refs[:6]
        cross_ref, *big_refs, design_buf, high_buf, low_buf, sems = refs[9:]
    else:
        table_ref, deg, order = refs[:3]
        cross_ref, *big_refs, pdeg, pord, design_buf, high_buf, low_buf, sems = refs[3:]

    @pl.when(pl.program_id(0) == 0)
    def _():
        if second:
            cross_ref[...] = cross_in[...]
            return
        cross_ref[...] = jnp.zeros_like(cross_ref)
        head = table_ref[0, :, TAB:WIDE].astype(F32)
        lanes = lax.broadcasted_iota(jnp.int32, (64, NDEG), 1).astype(F32)
        wide = lax.broadcasted_iota(jnp.int32, (64, NORD), 1).astype(F32)
        for k in range(NP // 64):
            d = head[:, 1 + k : 2 + k]
            o = head[:, 9 + k : 10 + k] * 2.0 + head[:, 17 + k : 18 + k]
            pdeg[64 * k : 64 * (k + 1), :] = (d == lanes).astype(BF16)
            pord[64 * k : 64 * (k + 1), :] = (o == wide).astype(BF16)

    last = ((1,), (1,))
    count = sems.shape[0]

    def writes(k):
        rows = pl.ds(k * sub, sub)
        return [
            pltpu.make_async_copy(buf.at[rows, :], ref.at[int(second), rows, :], sems.at[k, n])
            for n, (buf, ref) in enumerate(zip((design_buf, high_buf, low_buf), big_refs))
        ]

    def synthesize(k):
        rows = slice(k * sub, (k + 1) * sub)
        block = slice(k * sub // 64, (k + 1) * sub // 64)

        def columns(lo, hi):
            return table_ref[block, :, lo:hi].reshape(sub, hi - lo)

        lat, lon = columns(0, NDEG), columns(NDEG, TAB)
        weight = columns(TAB, WIDE).astype(F32)[:, 0:1]
        high, low = split(weight * dot(lat, pdeg[...], last) * dot(lon, pord[...], last))
        high_buf[rows, :], low_buf[rows, :] = high, low
        design = weight * dot(lat, deg[...]) * dot(lon, order[...])
        design_buf[rows, :] = design
        for write in writes(k):
            write.start()
        return high, low, split(design)

    def accumulate(high, low, design):
        lhs = jnp.concatenate([high.T, high.T, low.T], axis=1)
        cross_ref[...] += dot(lhs, jnp.concatenate([design[0], design[1], design[0]], axis=0))

    ready = synthesize(0)
    for k in range(count):
        following = synthesize(k + 1) if k + 1 < count else None
        accumulate(*ready)
        ready = following
    for k in range(count):
        for write in writes(k):
            write.wait()


def moments(table, deg, order, prior=None, sub=256):
    epochs, cols = 64 * table.shape[0], deg.shape[1]
    second = prior is not None
    whole = lambda i: (0, 0)
    here = pl.BlockSpec(memory_space=pltpu.VMEM)
    big_specs = [pl.BlockSpec(memory_space=pl.ANY)] * 3
    big_shapes = [
        pltpu.HBM((2, epochs, cols), F32),
        pltpu.HBM((2, epochs, NP), BF16),
        pltpu.HBM((2, epochs, NP), BF16),
    ]
    if second:
        cross, design, high, low, pdeg, pord = prior
        args = (table, deg, order, pdeg, pord, cross, *in_hbm(design, high, low))
        in_specs = [here] * 6 + [pl.BlockSpec(memory_space=pl.ANY)] * 3
        out_specs = [pl.BlockSpec((NP, cols), whole), *big_specs]
        out_shape = [pltpu.HBM((NP, cols), F32), *big_shapes]
        aliases = {6: 1, 7: 2, 8: 3}
    else:
        args = (table, deg, order)
        in_specs = [here] * 3
        out_specs = [here, *big_specs, here, here]
        out_shape = [
            pltpu.VMEM((NP, cols), F32),
            *big_shapes,
            pltpu.VMEM((NP, NDEG), BF16),
            pltpu.VMEM((NP, NORD), BF16),
        ]
        aliases = {}
    return pl.pallas_call(
        functools.partial(moments_kernel, second, sub),
        grid=(1,),
        in_specs=in_specs,
        out_specs=out_specs,
        out_shape=out_shape,
        scratch_shapes=[
            pltpu.VMEM((epochs, cols), F32),
            pltpu.VMEM((epochs, NP), BF16),
            pltpu.VMEM((epochs, NP), BF16),
            pltpu.SemaphoreType.DMA((epochs // sub, 3)),
        ],
        input_output_aliases=aliases,
        compiler_params=pltpu.CompilerParams(vmem_limit_bytes=VMEM_LIMIT),
        cost_estimate=pl.CostEstimate(
            flops=2 * epochs * (NP + cols) * TAB + 6 * epochs * cols * NP,
            bytes_accessed=epochs * (2 * WIDE + 4 * cols + 4 * NP),
            transcendentals=0,
        ),
        name="moments_second" if second else "moments_first",
    )(*args)


def slice_kernel(mine_ref, high_ref, low_ref, out_ref, total):
    first = (pl.program_id(0) == 0) & (pl.program_id(1) == 0)
    part = total.shape[0]
    row = mine_ref[0] * part + lax.broadcasted_iota(jnp.int32, (NP, part), 1)
    pick = (lax.broadcasted_iota(jnp.int32, (NP, part), 0) == row).astype(BF16)
    high, low = high_ref[0], low_ref[0]
    own_high, own_low = dot(high, pick).astype(BF16), dot(low, pick).astype(BF16)
    lhs = jnp.concatenate([own_high.T, own_high.T, own_low.T], axis=1)
    added = dot(lhs, jnp.concatenate([high, low, high], axis=0))

    @pl.when(first)
    def _():
        total[...] = added

    @pl.when(jnp.logical_not(first))
    def _():
        total[...] += added

    out_ref[...] = total[...]


def gram_slice(mine, high, low, part, rows=1024):
    halves, epochs = high.shape[:2]
    spec = pl.BlockSpec((1, rows, NP), lambda h, i, s: (h, i, 0))
    return pl.pallas_call(
        slice_kernel,
        grid_spec=pltpu.PrefetchScalarGridSpec(
            num_scalar_prefetch=1,
            grid=(halves, epochs // rows),
            in_specs=[spec, spec],
            out_specs=pl.BlockSpec((part, NP), lambda h, i, s: (0, 0)),
            scratch_shapes=[pltpu.VMEM((part, NP), F32)],
        ),
        out_shape=jax.ShapeDtypeStruct((part, NP), F32),
        compiler_params=pltpu.CompilerParams(vmem_limit_bytes=SMALL_VMEM),
        cost_estimate=pl.CostEstimate(
            flops=12 * epochs * part * NP, bytes_accessed=8 * epochs * NP, transcendentals=0
        ),
        name="gram_slice",
    )(mine, *in_hbm(high, low))


def invert_block(s_ref, t_ref, x_ref):
    full = (GROUP, NB)
    for g in range(NB // GROUP):
        lo = GROUP * g
        rows = [jnp.broadcast_to(s_ref[lo + i : lo + i + 1, :], full) for i in range(GROUP)]
        extra = [jnp.broadcast_to(t_ref[lo + i : lo + i + 1, :], full) for i in range(GROUP)]
        s = [[jnp.broadcast_to(rows[i][:, lo + j : lo + j + 1], full) for j in range(i + 1)] for i in range(GROUP)]
        inv = [None] * GROUP
        mult = [[None] * GROUP for _ in range(GROUP)]
        for p in range(GROUP):
            inv[p] = 1.0 / s[p][p]
            for i in range(p + 1, GROUP):
                mult[i][p] = s[i][p] * inv[p]
            for i in range(p + 1, GROUP):
                for j in range(p + 1, i + 1):
                    s[i][j] = s[i][j] - mult[i][p] * s[j][p]
            for i in range(p + 1, GROUP):
                rows[i] = rows[i] - mult[i][p] * rows[p]
                extra[i] = extra[i] - mult[i][p] * extra[p]
        for i in range(GROUP):
            x_ref[lo + i : lo + i + 1, :] = (lax.rsqrt(s[i][i]) * extra[i])[0:1, :]
        if g == NB // GROUP - 1:
            break
        y = [r * v for r, v in zip(rows, inv)]
        z = [e * v for e, v in zip(extra, inv)]
        for i in range(GROUP - 1, 0, -1):
            for m in range(i):
                y[m] = y[m] - mult[i][m] * y[i]
                z[m] = z[m] - mult[i][m] * z[i]
        for h in range(g + 1, NB // GROUP):
            at = slice(GROUP * h, GROUP * (h + 1))
            tile = s_ref[at, :]
            other = t_ref[at, :]
            for m in range(GROUP):
                col = jnp.broadcast_to(tile[:, lo + m : lo + m + 1], full)
                if m == 0:
                    da, db = col * y[m], col * z[m]
                else:
                    da, db = da + col * y[m], db + col * z[m]
            s_ref[at, :] = tile - da
            t_ref[at, :] = other - db


def factor_kernel(gram_ref, out_ref, a_ref, s_ref, t_ref, x_ref):
    cores, planes, part = gram_ref.shape[:3]
    for p in range(planes):
        for c in range(cores):
            at = part * (cores * p + c)
            a_ref[at : at + part, :] = gram_ref[c, p]
    out_ref[...] = jnp.zeros_like(out_ref)
    unit = (
        lax.broadcasted_iota(jnp.int32, (NB, NB), 0) == lax.broadcasted_iota(jnp.int32, (NB, NB), 1)
    ).astype(F32)
    count = NP // NB

    @pl.loop(0, count)
    def _(k):
        for i in range(count):

            @pl.when(k == i)
            def _():
                at = slice(NB * i, NB * (i + 1))
                s_ref[...] = a_ref[at, at]

        t_ref[...] = unit
        invert_block(s_ref, t_ref, x_ref)
        for i in range(count):

            @pl.when(k == i)
            def _():
                at = slice(NB * i, NB * (i + 1))
                x = x_ref[...]
                out_ref[at, at] = x
                if i > 0:
                    done = slice(0, NB * i)
                    out_ref[at, done] = dot(x, out_ref[at, done], precision=HIGHEST)
                if i < count - 1:
                    rest = slice(NB * (i + 1), NP)
                    upper = dot(x, a_ref[at, rest], precision=HIGHEST)
                    a_ref[rest, rest] -= dot(upper, upper, ((0,), (0,)), HIGHEST)
                    done = slice(0, NB * (i + 1))
                    out_ref[rest, done] -= dot(upper, out_ref[at, done], ((0,), (0,)), HIGHEST)


def inverse_factor(gram):
    return pl.pallas_call(
        factor_kernel,
        out_shape=jax.ShapeDtypeStruct((NP, NP), F32),
        scratch_shapes=[pltpu.VMEM((NP, NP), F32)] + [pltpu.VMEM((NB, NB), F32)] * 3,
        compiler_params=pltpu.CompilerParams(vmem_limit_bytes=SMALL_VMEM),
        cost_estimate=pl.CostEstimate(flops=300_000_000, bytes_accessed=2 * 4 * NP * NP, transcendentals=0),
        name="inverse_factor",
    )(gram)


def basis_kernel(inv_ref, high_ref, low_ref, qhigh_ref, qlow_ref, xhigh_ref, xlow_ref):
    @pl.when((pl.program_id(0) == 0) & (pl.program_id(1) == 0))
    def _():
        xhigh_ref[...], xlow_ref[...] = split(inv_ref[...])

    last = ((1,), (1,))
    high, xhigh = high_ref[0], xhigh_ref[...]
    basis = dot(high, xhigh, last) + dot(high, xlow_ref[...], last) + dot(low_ref[0], xhigh, last)
    qhigh_ref[0], qlow_ref[0] = split(basis)


def basis_of(inv, high, low, rows=512):
    halves, epochs = high.shape[:2]
    spec = pl.BlockSpec((1, rows, NP), lambda h, i: (h, i, 0))
    whole = pl.BlockSpec((NP, NP), lambda h, i: (0, 0))
    return pl.pallas_call(
        basis_kernel,
        grid=(halves, epochs // rows),
        in_specs=[whole, spec, spec],
        out_specs=[spec, spec, whole, whole],
        out_shape=[pltpu.VMEM(high.shape, BF16), pltpu.HBM(high.shape, BF16)] + [pltpu.VMEM((NP, NP), BF16)] * 2,
        compiler_params=pltpu.CompilerParams(vmem_limit_bytes=SMALL_VMEM),
        cost_estimate=pl.CostEstimate(
            flops=12 * epochs * NP * NP, bytes_accessed=16 * epochs * NP, transcendentals=0
        ),
        name="basis_of",
    )(inv, *in_hbm(high, low))


def project_kernel(core_ref, xhigh, xlow, qhigh, cross_ref, qlow_ref, design_ref, coef_hbm, rest_ref,
                   coef_ref, both, sem):
    h, i = pl.program_id(0), pl.program_id(1)
    put = pltpu.make_async_copy(coef_ref, coef_hbm, sem)

    @pl.when((h == 0) & (i == 0))
    def _():
        high, low = split(cross_ref[...])
        half = NP // 2
        for rows, depth in ((slice(0, half), half), (slice(half, NP), NP)):
            left = [x[rows, 0:depth] for x in (xhigh, xhigh, xlow)]
            right = [x[0:depth] for x in (high, low, high)]
            coef_ref[rows, :] = dot(jnp.concatenate(left, axis=1), jnp.concatenate(right, axis=0))
        put.start()
        both[0:NP, :], both[NP : 2 * NP, :] = split(coef_ref[...])

    rows = design_ref.shape[1]
    high = qhigh[h, pl.ds(pl.multiple_of(i * rows, rows), rows), :]
    span = dot(jnp.concatenate([high, high], axis=1), both[...]) + dot(qlow_ref[0], both[0:NP, :])
    rest_ref[...] = (design_ref[0] - span).reshape(rest_ref.shape)

    @pl.when((h == pl.num_programs(0) - 1) & (i == pl.num_programs(1) - 1))
    def _():
        put.wait()


def project(core, xhigh, xlow, cross, high, low, design, rows=512):
    halves, epochs, cols = design.shape
    here = pl.BlockSpec(memory_space=pltpu.VMEM)
    whole = pl.BlockSpec((NP, cols), lambda h, i, s: (0, 0))
    along = lambda h, i, s: (h, i, 0)
    return pl.pallas_call(
        project_kernel,
        grid_spec=pltpu.PrefetchScalarGridSpec(
            num_scalar_prefetch=1,
            grid=(halves, epochs // rows),
            in_specs=[
                here,
                here,
                here,
                whole,
                pl.BlockSpec((1, rows, NP), along),
                pl.BlockSpec((1, rows, cols), along),
            ],
            out_specs=[
                pl.BlockSpec(memory_space=pl.ANY),
                pl.BlockSpec((rows // 64, 1, 64, cols), lambda h, i, s: (i, (s[0] + h) % 2, 0, 0)),
            ],
            scratch_shapes=[
                pltpu.VMEM((NP, cols), F32),
                pltpu.VMEM((2 * NP, cols), BF16),
                pltpu.SemaphoreType.DMA,
            ],
        ),
        out_shape=[
            pltpu.HBM((NP, cols), F32),
            jax.ShapeDtypeStruct((epochs // 64, halves, 64, cols), F32),
        ],
        compiler_params=pltpu.CompilerParams(vmem_limit_bytes=VMEM_LIMIT),
        cost_estimate=pl.CostEstimate(
            flops=12 * epochs * cols * NP, bytes_accessed=2 * epochs * (8 * cols + 4 * NP), transcendentals=0
        ),
        name="project",
    )(core, xhigh, xlow, high, *in_hbm(cross, low, design))


def copies(x, count):
    return jnp.broadcast_to(x[None], (count, *x.shape))


def shards(latitude, longitude, weight, harmonic_index):
    plane, cores, nrow = ("x", "y"), lax.axis_size("core"), lax.axis_size("row")
    places = lax.axis_size("x") * lax.axis_size("y")
    core = lax.axis_index("core")
    mine = (lax.axis_index(plane) * cores + core).reshape(1)
    lead = lax.all_gather(harmonic_index, "core")
    packed = pack(latitude, longitude, weight, lead, places)
    deg, order = onehots(harmonic_index)
    own = lax.all_to_all(packed, plane, 0, 0)
    other = lax.ppermute(own, "core", [(k, (k + 1) % cores) for k in range(cores)])
    part = NP // (places * cores)
    cross, design, high, low = moments(other, deg, order, moments(own, deg, order))
    cross = lax.psum(cross, "row")
    summed = gram_slice(mine, high, low, part)
    hop = 1
    while hop < nrow:
        summed = summed + lax.ppermute(summed, "row", [(k, k ^ hop) for k in range(nrow)])
        hop *= 2
    near = lax.all_to_all(copies(summed, places), plane, 0, 0)
    gram = lax.all_to_all(copies(near, cores), "core", 0, 0)
    inv = inverse_factor(gram)
    qhigh, qlow, xhigh, xlow = basis_of(inv, high, low)
    coefficients, rest = project(core.reshape(1), xhigh, xlow, cross, qhigh, qlow, design)
    return coefficients, rest.reshape(-1, rest.shape[-1])


def solution(mesh):
    sizes = dict(mesh.shape)
    side = int(round((sizes["col"] // 2) ** 0.5))
    fine = Mesh(
        mesh.devices.reshape(sizes["row"], side, sizes["col"] // (2 * side), 2), ("row", "x", "y", "core")
    )
    col = ("x", "y", "core")
    every = ("row", *col)
    return jax.shard_map(
        shards,
        mesh=fine,
        in_specs=(P(every, None), P(every, None), P(every), P(None, col)),
        out_specs=(P(None, col), P("row", col)),
        check_vma=False,
    )
```
